32 devices in a mesh: dp: 2 (over y), row: 4 (over z), col: 4 (over x, core).
Axes of the slice: x: 2, y: 2, z: 4, core: 2. Of those that a mesh axis runs over, the one named last changes fastest.
Arguments:
- hidden_in: float32 [2048, 1024], P(('dp', 'col'), 'row'), may hold values from -6 to 6
- segments: int32 [2, 1024], P('dp'), may hold values from 0 to 2, never falling along the last dimension, each value on 1 to 600 neighbouring positions
- norm_in: float32 [1024], P('row'), may hold values from 0.5 to 1.5
- w_query: bfloat16 [1024, 1024], P('row', 'col'), may hold values from -0.1875 to 0.1875
- w_key: bfloat16 [1024, 512], P('row', 'col'), may hold values from -0.1875 to 0.1875
- w_value: bfloat16 [1024, 512], P('row', 'col'), may hold values from -0.1875 to 0.1875
- query_gain: float32 [64], replicated, may hold values from 0.5 to 1.5
- key_gain: float32 [64], replicated, may hold values from 0.5 to 1.5
- w_out: bfloat16 [1024, 1024], P('col', 'row'), may hold values from -0.75 to 0.75
- norm_mid: float32 [1024], P('row'), may hold values from 0.5 to 1.5
- w_gate: bfloat16 [1024, 4608], P('row', 'col'), may hold values from -0.1875 to 0.1875
- w_up: bfloat16 [1024, 4608], P('row', 'col'), may hold values from -0.1875 to 0.1875
- w_down: bfloat16 [4608, 1024], P('col', 'row'), may hold values from -0.15625 to 0.15625
- cotangent: float32 [2048, 1024], P(('dp', 'col'), 'row'), may hold values from -6 to 6
Outputs:
- output: float32 [2048, 1024], P(('dp', 'col'), 'row')
- grad_hidden: float32 [2048, 1024], P(('dp', 'col'), 'row')
- grad_norm_in: float32 [1024], P('row')
- grad_query: float32 [1024, 1024], P('row', 'col')
- grad_key: float32 [1024, 512], P('row', 'col')
- grad_value: float32 [1024, 512], P('row', 'col')
- grad_query_gain: float32 [64], replicated
- grad_key_gain: float32 [64], replicated
- grad_out: float32 [1024, 1024], P('col', 'row')
- grad_norm_mid: float32 [1024], P('row')
- grad_gate: float32 [1024, 4608], P('row', 'col')
- grad_up: float32 [1024, 4608], P('row', 'col')
- grad_down: float32 [4608, 1024], P('col', 'row')
The draws below stay inside these ranges and needn't reach their ends.
Inputs may be any that keep to these rules, and one draw needn't show every extreme that they name: `segments`: within each row the numbers never fall; each of the 3 documents has 1 to 600 tokens, and one has exactly 600.
All inputs are finite; a program needn't handle non-finite values.
Results may differ from the reference program's by a relative error of at most 0.017.
Values may be sent and summed in bfloat16 or wider, within the bound.
A program may use at most 128 MiB of HBM per device.

```python
import math
import jax
import jax.numpy as jnp
import numpy as np
from jax import lax

D = 1024
HEADS = 16
KV_HEADS = 8
HEAD_DIM = 64
FF = 4608
LEN = 1024
SEGS = 3
DOC_MOST = 600
N_SEQ = 2
TOKENS = 2048


def level_of(stream_key, shape, shards, smallest, largest):
    def one(dim, shards_of):
        heights = jax.random.uniform(jax.random.fold_in(jax.random.fold_in(stream_key, 6), dim), (shards_of,), jnp.float32, smallest / len(shards), largest / len(shards))
        return jnp.repeat(jnp.exp(heights), shape[dim] // shards_of).reshape((-1,) + (1,) * (len(shape) - dim - 1))

    factor_of = one(*shards[0])
    for cut in shards[1:]:
        factor_of = factor_of * one(*cut)
    return factor_of


def split_up(count, total, limit, slope):
    portions = [(1 << 20) // math.isqrt(standing ** slope) + 1 for standing in range(2, count + 1)]
    surplus, given = total - limit - (count - 1), [1] * (count - 1)
    while surplus > 0:
        movable = [i for i in range(count - 1) if given[i] < limit]
        whole, left = sum([portions[i] for i in movable]), surplus
        for i in movable:
            extra = min(limit - given[i], max(1, left * portions[i] // whole), surplus)
            given[i] = given[i] + extra
            surplus = surplus - extra
    return np.array([limit] + given)


def ragged(rng, amount, total, bound, skew):
    if amount == 2:
        one = jax.random.randint(rng, (), max(1, total - bound), min(bound, total - 1) + 1)
        return jnp.stack([one, total - one])
    tallies = jnp.asarray(split_up(amount, total, bound, skew), jnp.int32)
    twos = (amount - 1) // 2
    source_of, receiver = tallies[1:1 + 2 * twos:2], tallies[2:2 + 2 * twos:2]
    slack = jnp.minimum(source_of - 1, bound - receiver)
    passed = jax.random.randint(jax.random.fold_in(rng, 1), (twos,), 0, 1 << 20) % (slack + 1)
    tallies = tallies.at[1:1 + 2 * twos:2].set(source_of - passed).at[2:2 + 2 * twos:2].set(receiver + passed)
    return tallies[jax.random.permutation(jax.random.fold_in(rng, 2), amount)]


def scatter_about(rng, dims, scale, most, cuts=(), kind=jnp.bfloat16):
    result = scale * jax.random.normal(rng, dims, jnp.float32)
    if cuts:
        result = result * level_of(rng, dims, cuts, -0.22, 0.18)
    return jnp.clip(result, -most, most).astype(kind)


def setup_inputs(seed: int = 0) -> dict:
    streams_of = jax.random.split(jax.random.key(seed), 15)
    hidden_in = scatter_about(streams_of[0], (TOKENS, D), 1.0, 6.0, ((0, 8), (1, 4)), jnp.float32)
    segments = jax.vmap(lambda own: jnp.searchsorted(jnp.cumsum(ragged(own, SEGS, LEN, DOC_MOST, 1)), jnp.arange(LEN), side="right"))(jax.random.split(streams_of[1], N_SEQ)).reshape((N_SEQ, LEN)).astype(jnp.int32)
    norm_in = jnp.clip(1.0 + 0.1 * jax.random.normal(streams_of[2], (D,), jnp.float32), 0.5, 1.5)
    w_query = scatter_about(streams_of[3], (D, HEADS * HEAD_DIM), D ** -0.5, 0.1875, ((0, 4), (1, 4)))
    w_key = scatter_about(streams_of[4], (D, KV_HEADS * HEAD_DIM), D ** -0.5, 0.1875, ((0, 4), (1, 4)))
    w_value = scatter_about(streams_of[5], (D, KV_HEADS * HEAD_DIM), D ** -0.5, 0.1875, ((0, 4), (1, 4)))
    query_gain = jnp.clip(1.0 + 0.1 * jax.random.normal(streams_of[6], (HEAD_DIM,), jnp.float32), 0.5, 1.5)
    key_gain = jnp.clip(1.0 + 0.1 * jax.random.normal(streams_of[7], (HEAD_DIM,), jnp.float32), 0.5, 1.5)
    w_out = scatter_about(streams_of[8], (HEADS * HEAD_DIM, D), (HEADS * HEAD_DIM // 16) ** -0.5, 0.75, ((0, 4), (1, 4)))
    norm_mid = jnp.clip(1.0 + 0.1 * jax.random.normal(streams_of[9], (D,), jnp.float32), 0.5, 1.5)
    w_gate = scatter_about(streams_of[10], (D, FF), D ** -0.5, 0.1875, ((0, 4), (1, 4)))
    w_up = scatter_about(streams_of[11], (D, FF), D ** -0.5, 0.1875, ((0, 4), (1, 4)))
    w_down = scatter_about(streams_of[12], (FF, D), (FF // 3) ** -0.5, 0.15625, ((0, 4), (1, 4)))
    cotangent = scatter_about(streams_of[13], (TOKENS, D), 1.0, 6.0, ((0, 8), (1, 4)), jnp.float32)
    return dict(hidden_in=hidden_in, segments=segments, norm_in=norm_in, w_query=w_query, w_key=w_key, w_value=w_value, query_gain=query_gain, key_gain=key_gain, w_out=w_out, norm_mid=norm_mid, w_gate=w_gate, w_up=w_up, w_down=w_down, cotangent=cotangent)


epsilon = 1e-05
rope_base = 1000000.0

def positions_of(documents):
    length = documents.shape[0]
    places = jnp.arange(length, dtype=jnp.int32)
    starts_here = jnp.concatenate([places[:1] >= 0, documents[1:] != documents[:-1]])
    doc_start = lax.cummax(jnp.where(starts_here, places, 0).astype(jnp.int32), axis=0)
    return places - doc_start

def rotary_tables(positions):
    half_dim = HEAD_DIM // 2
    frequency = rope_base ** (-2.0 * jnp.arange(half_dim, dtype=jnp.float32) / HEAD_DIM)
    angles = positions.astype(jnp.float32)[:, None] * frequency[None, :]
    return (jnp.cos(angles)[:, None, :], jnp.sin(angles)[:, None, :])

def rotate(values, cos_table, sin_table):
    half_dim = HEAD_DIM // 2
    first_half, second = (values[..., :half_dim], values[..., half_dim:])
    return jnp.concatenate([first_half * cos_table - second * sin_table, second * cos_table + first_half * sin_table], axis=-1)

def rotate_back(gradient, cos_table, sin_table):
    half_dim = HEAD_DIM // 2
    first_half, second = (gradient[..., :half_dim], gradient[..., half_dim:])
    return jnp.concatenate([first_half * cos_table + second * sin_table, second * cos_table - first_half * sin_table], axis=-1)

def head_rates(values):
    return lax.rsqrt(lax.optimization_barrier(jnp.mean(values * values, axis=-1, keepdims=True)) + epsilon)

def head_back(values, rate_rows, gain, gradient):
    scaled = gain * gradient
    inner_mean = lax.optimization_barrier(jnp.mean(scaled * values, axis=-1, keepdims=True))
    return (rate_rows * scaled - values * rate_rows ** 3 * inner_mean, lax.optimization_barrier(jnp.sum(gradient * values * rate_rows, axis=(0, 1))))

def one_sequence(hidden, cotan, documents, weights):
    norm_in, w_query, w_key, w_value, query_gain, key_gain, w_out, norm_mid, w_gate, w_up, w_down = weights
    length = hidden.shape[0]
    q_cols = HEADS * HEAD_DIM
    k_cols = KV_HEADS * HEAD_DIM
    groups = HEADS // KV_HEADS
    scale_factor = HEAD_DIM ** (-0.5)
    flt = jnp.float32
    low = jnp.bfloat16
    rate_in = lax.rsqrt(lax.optimization_barrier(jnp.mean(hidden * hidden, axis=1, keepdims=True)) + epsilon)
    normed_in = (hidden * rate_in * norm_in).astype(low)
    w_joined = jnp.concatenate([w_query, w_key, w_value], axis=1)
    projected = jnp.dot(normed_in, w_joined, preferred_element_type=flt)
    raw_query = projected[:, :q_cols].reshape(length, HEADS, HEAD_DIM)
    raw_key = projected[:, q_cols:q_cols + k_cols].reshape(length, KV_HEADS, HEAD_DIM)
    value_low = projected[:, q_cols + k_cols:].astype(low)
    cos_table, sin_table = rotary_tables(positions_of(documents))
    query_rate = head_rates(raw_query)
    key_rate = head_rates(raw_key)
    query_rot = rotate(raw_query * query_rate * query_gain, cos_table, sin_table).astype(low)
    key_rot = rotate(raw_key * key_rate * key_gain, cos_table, sin_table).astype(low)
    places = jnp.arange(length, dtype=jnp.int32)
    allowed = (documents[:, None] == documents[None, :]) & (places[:, None] >= places[None, :])
    query_blocks = query_rot.reshape(length, KV_HEADS, groups, HEAD_DIM).astype(flt)
    key_heads = key_rot.astype(flt)
    value_heads = value_low.reshape(length, KV_HEADS, HEAD_DIM).astype(flt)
    scores = jnp.einsum('qkgd,skd->kgqs', query_blocks, key_heads) * scale_factor
    log_total = jnp.log(lax.optimization_barrier(jnp.sum(jnp.where(allowed, jnp.exp(scores), 0.0), axis=-1, keepdims=True)))
    probability = jnp.where(allowed, jnp.exp(scores - log_total), 0.0)
    prob_low = probability.astype(low).astype(flt)
    mixed = jnp.einsum('kgqs,skd->qkgd', prob_low, value_heads).reshape(length, q_cols).astype(low)
    resid = hidden + jnp.dot(mixed, w_out, preferred_element_type=flt)
    rate_mid = lax.rsqrt(lax.optimization_barrier(jnp.mean(resid * resid, axis=1, keepdims=True)) + epsilon)
    normed_mid = (resid * rate_mid * norm_mid).astype(low)
    gate_pre = jnp.dot(normed_mid, w_gate, preferred_element_type=flt)
    up_pre = jnp.dot(normed_mid, w_up, preferred_element_type=flt)
    sigmoid_gate = jax.nn.sigmoid(gate_pre)
    activated = gate_pre * sigmoid_gate
    swiglu = (activated * up_pre).astype(low)
    output = resid + jnp.dot(swiglu, w_down, preferred_element_type=flt)
    cot_low = cotan.astype(low)
    grad_down = jnp.dot(swiglu.T, cot_low, preferred_element_type=flt)
    grad_swiglu = jnp.dot(cot_low, w_down.T, preferred_element_type=flt)
    grad_gate_act = (grad_swiglu * up_pre * sigmoid_gate * (1.0 + gate_pre * (1.0 - sigmoid_gate))).astype(low)
    grad_up_act = (grad_swiglu * activated).astype(low)
    grad_gate = jnp.dot(normed_mid.T, grad_gate_act, preferred_element_type=flt)
    grad_up = jnp.dot(normed_mid.T, grad_up_act, preferred_element_type=flt)
    grad_normed_mid = jnp.dot(grad_gate_act, w_gate.T, preferred_element_type=flt) + jnp.dot(grad_up_act, w_up.T, preferred_element_type=flt)
    scaled_mid = norm_mid * grad_normed_mid
    grad_resid = cotan + rate_mid * scaled_mid - resid * rate_mid ** 3 * lax.optimization_barrier(jnp.mean(scaled_mid * resid, axis=1, keepdims=True))
    grad_norm_mid = lax.optimization_barrier(jnp.sum(grad_normed_mid * resid * rate_mid, axis=0))
    resid_low = grad_resid.astype(low)
    grad_out = jnp.dot(mixed.T, resid_low, preferred_element_type=flt)
    grad_mixed = jnp.dot(resid_low, w_out.T, preferred_element_type=flt).astype(low)
    grad_mixed_heads = grad_mixed.reshape(length, KV_HEADS, groups, HEAD_DIM).astype(flt)
    grad_value_act = jnp.einsum('kgqs,qkgd->skd', prob_low, grad_mixed_heads)
    grad_probs = jnp.einsum('qkgd,skd->kgqs', grad_mixed_heads, value_heads)
    row_inner = lax.optimization_barrier(jnp.sum(probability * grad_probs, axis=-1, keepdims=True))
    grad_scores = (probability * (grad_probs - row_inner) * scale_factor).astype(low).astype(flt)
    grad_query_rot = jnp.einsum('kgqs,skd->qkgd', grad_scores, key_heads).reshape(length, HEADS, HEAD_DIM)
    grad_key_rot = jnp.einsum('kgqs,qkgd->skd', grad_scores, query_blocks)
    grad_raw_query, grad_query_gain = head_back(raw_query, query_rate, query_gain, rotate_back(grad_query_rot, cos_table, sin_table))
    grad_raw_key, grad_key_gain = head_back(raw_key, key_rate, key_gain, rotate_back(grad_key_rot, cos_table, sin_table))
    grad_proj = jnp.concatenate([grad_raw_query.reshape(length, q_cols), grad_raw_key.reshape(length, k_cols), grad_value_act.reshape(length, k_cols)], axis=1).astype(low)
    grad_joined = jnp.dot(normed_in.T, grad_proj, preferred_element_type=flt)
    grad_normed_in = jnp.dot(grad_proj, w_joined.T, preferred_element_type=flt)
    scaled_in = norm_in * grad_normed_in
    grad_hidden = grad_resid + rate_in * scaled_in - hidden * rate_in ** 3 * lax.optimization_barrier(jnp.mean(scaled_in * hidden, axis=1, keepdims=True))
    grad_norm_in = lax.optimization_barrier(jnp.sum(grad_normed_in * hidden * rate_in, axis=0))
    gradients = (grad_norm_in, grad_joined[:, :q_cols], grad_joined[:, q_cols:q_cols + k_cols], grad_joined[:, q_cols + k_cols:], grad_query_gain, grad_key_gain, grad_out, grad_norm_mid, grad_gate, grad_up, grad_down)
    return (output, grad_hidden, gradients)

def reference(hidden_in, segments, norm_in, w_query, w_key, w_value, query_gain, key_gain, w_out, norm_mid, w_gate, w_up, w_down, cotangent):
    weights = (norm_in, w_query, w_key, w_value, query_gain, key_gain, w_out, norm_mid, w_gate, w_up, w_down)
    totals = tuple((jnp.zeros(weight.shape, jnp.float32) for weight in weights))
    stacked = (hidden_in.reshape(N_SEQ, LEN, D), cotangent.reshape(N_SEQ, LEN, D), segments)

    def advance(carried, item):
        hidden, cotan, documents = item
        output, grad_hidden, gradients = one_sequence(hidden, cotan, documents, weights)
        return (jax.tree.map(lambda left_side, right_side: left_side + right_side, carried, gradients), (output, grad_hidden))
    totals, (outputs, grad_rows) = lax.scan(advance, totals, stacked)
    return (outputs.reshape(TOKENS, D), grad_rows.reshape(TOKENS, D), totals[0], totals[1], totals[2], totals[3], totals[4], totals[5], totals[6], totals[7], totals[8], totals[9], totals[10])
```

```python
import functools
from types import SimpleNamespace

import jax
import jax.numpy as jnp
from jax import lax
from jax.experimental import pallas as pl
from jax.experimental.pallas import tpu as pltpu
from jax.sharding import PartitionSpec as P

HEAD_DIM = 64
epsilon = 1e-05
rope_base = 1000000.0
LOW = jnp.bfloat16
FLT = jnp.float32
ORDER = (1, 3, 2)


def nn(left_side, right_side):
    return jnp.dot(left_side, right_side, preferred_element_type=FLT)


def nt(left_side, right_side):
    return lax.dot_general(
        left_side, right_side, (((1,), (1,)), ((), ())), preferred_element_type=FLT
    )


def row_sums(block):
    return jnp.sum(jnp.transpose(block), axis=0, keepdims=True)


def to_column(row):
    return jnp.transpose(jnp.broadcast_to(row, (128, row.shape[1])))[:, :1]


def to_row(column):
    return jnp.transpose(jnp.broadcast_to(column, (column.shape[0], 128)))[:1, :]


class Node:
    def __init__(self, pair):
        self.pair = pair
        self.r = lax.axis_index("row")
        self.c = lax.axis_index("col")
        self.d = lax.axis_index("dp")
        self.near = self.c + 1 - 2 * lax.rem(self.c, 2)
        self.far = lax.rem(self.c + 2, 4)
        self.across = lax.rem(self.near + 2, 4)

    def row(self, step):
        return lax.rem(self.r + step, 4)

    def send(self, src, dst, sems, slot, **where):
        copy = pltpu.make_async_remote_copy(
            src_ref=src,
            dst_ref=dst,
            send_sem=sems[0].at[slot],
            recv_sem=sems[1].at[slot],
            device_id=where,
            device_id_type=pl.DeviceIdType.MESH,
        )
        copy.start()
        return copy

    def group(self):
        places = []
        for dp_step in range(2 if self.pair else 1):
            for col_step in range(4):
                if dp_step + col_step:
                    where = {"col": lax.rem(self.c + col_step, 4)}
                    if self.pair:
                        where["dp"] = lax.rem(self.d + dp_step, 2)
                    places.append(where)
        return places

    def group_slot(self):
        return self.d * 4 + self.c if self.pair else self.c


def span(block, size):
    return pl.ds(pl.multiple_of(block * size, size), size)


def gather_steps(node, whole, sems, done=None):
    size = whole.shape[1] // 4
    mine = span(node.c, size)

    def here(r, c):
        return whole.at[r, span(c, size)]

    def spread(i, r):
        block = here(r, node.c)
        return (
            node.send(block, block, sems, 3 + i, col=node.near),
            node.send(block, block, sems, 7 + i, col=node.far),
        )

    own = whole.at[node.r, mine]
    along = [node.send(own, own, sems, s - 1, row=node.row(s)) for s in (1, 2, 3)]
    rows = [node.r] + [lax.rem(node.r + 4 - s, 4) for s in ORDER]
    near, far, relay = {}, {}, {}

    def pass_on(i):
        far[i].wait_recv()
        block = here(rows[i], node.far)
        relay[i] = node.send(block, block, sems, 11 + i, col=node.near)

    def complete(i):
        near[i].wait_recv()
        relay[i].wait_recv()
        if done is not None:
            done(rows[i], i)

    near[0], far[0] = spread(0, rows[0])
    yield
    for i in (1, 2, 3):
        along[ORDER[i - 1] - 1].wait_recv()
        near[i], far[i] = spread(i, rows[i])
        pass_on(i - 1)
        yield
        if i >= 2:
            complete(i - 2)
            yield
    pass_on(3)
    complete(2)
    yield
    complete(3)
    yield
    for copy in along + list(near.values()) + list(far.values()) + list(relay.values()):
        copy.wait_send()


def reduce_steps(node, bufs, sems, compute, finish):
    part, got, passed, from_far, out, arrived = bufs
    size = part.shape[1] // 4
    steps = (2, 1, 3, 0)
    rows = [node.row(s) for s in steps]
    first, second, crossing, along = {}, {}, {}, {}
    state = {}

    def begin(i):
        compute(rows[i])
        first[i] = node.send(
            part.at[rows[i], span(node.across, size)], got.at[i, 0], sems, i, col=node.near
        )
        second[i] = node.send(
            part.at[rows[i], span(node.near, size)], got.at[i, 1], sems, 4 + i, col=node.near
        )

    def cross(i):
        first[i].wait_recv()
        passed[i] = (
            part[rows[i], span(node.far, size)].astype(FLT) + got[i, 0].astype(FLT)
        ).astype(LOW)
        crossing[i] = node.send(passed.at[i], from_far.at[i], sems, 8 + i, col=node.far)

    def close(i):
        second[i].wait_recv()
        crossing[i].wait_recv()
        total = (
            part[rows[i], span(node.c, size)].astype(FLT)
            + got[i, 1].astype(FLT)
            + from_far[i].astype(FLT)
        )
        if steps[i]:
            out[i] = total.astype(LOW)
            along[i] = node.send(out.at[i], arrived.at[i], sems, 12 + i, row=rows[i])
        else:
            state["own"] = total

    for i in range(4):
        begin(i)
        if i >= 1:
            cross(i - 1)
        if i >= 2:
            close(i - 2)
        yield
    cross(3)
    close(2)
    yield
    close(3)
    total = state["own"]
    for i in range(3):
        along[i].wait_recv()
        total = total + arrived[i].astype(FLT)
    finish(total)
    yield
    for group in (first, second, crossing, along):
        for copy in group.values():
            copy.wait_send()


def weight_steps(node, src, dst, sems, own_sem):
    rows = src.shape[1]
    own = pltpu.make_async_copy(src.at[node.r], dst.at[node.r], own_sem)
    own.start()
    half = rows // 2 if node.pair else rows
    mine = span(node.d, half) if node.pair else pl.ds(0, rows)
    along = {
        s: node.send(src.at[node.row(s), mine], dst.at[node.r, mine], sems, s - 1, row=node.row(s))
        for s in ORDER
    }
    yield
    over = []
    for i, s in enumerate(ORDER):
        along[s].wait_recv()
        if node.pair:
            block = dst.at[lax.rem(node.r + 4 - s, 4), mine]
            over.append(node.send(block, block, sems, 3 + i, dp=1 - node.d))
    yield
    own.wait()
    for copy in over:
        copy.wait_recv()
    yield
    for copy in list(along.values()) + over:
        copy.wait_send()


def grad_steps(node, src, partner, total, dst, sems, start):
    rows = src.shape[1]
    start()
    if node.pair:
        half = rows // 2
        mine, other = span(node.d, half), span(1 - node.d, half)
        over = node.send(src.at[:, other], partner, sems, 0, dp=1 - node.d)
        yield
        over.wait_recv()
    else:
        mine = pl.ds(0, rows)
        yield

    def fill(i, _):
        value = src[i, mine]
        if node.pair:
            value = (value.astype(FLT) + partner[i].astype(FLT)).astype(LOW)
        total[i] = value
        return 0

    lax.fori_loop(0, 4, fill, 0)
    along = {
        s: node.send(total.at[node.row(s)], dst.at[node.r, mine], sems, s, row=node.row(s))
        for s in ORDER
    }
    dst[node.r, mine] = total[node.r]
    yield
    for s in ORDER:
        along[s].wait_recv()
    if node.pair:
        back = node.send(dst.at[:, mine], dst.at[:, mine], sems, 4, dp=1 - node.d)
        yield
        back.wait_recv()
    yield
    for copy in along.values():
        copy.wait_send()
    if node.pair:
        over.wait_send()
        back.wait_send()


def row_stat_steps(node, box, sums, sems):
    box[node.r] = jnp.broadcast_to(sums, box.shape[1:])
    copies = [
        node.send(box.at[node.r], box.at[node.r], sems, s - 1, row=node.row(s)) for s in (1, 2, 3)
    ]
    for copy in copies:
        copy.wait_recv()
    total = box[0] + box[1] + box[2] + box[3]
    for copy in copies:
        copy.wait_send()
    return total[0:1]


def group_sum_start(node, box, value, sems):
    slot = node.group_slot()
    box[slot] = value
    return [
        node.send(box.at[slot], box.at[slot], sems, i, **where)
        for i, where in enumerate(node.group())
    ]


def box_total(box):
    total = box[0]
    for i in range(1, box.shape[0]):
        total = total + box[i]
    return total


def kernel(dims, pair, names, *refs):
    k = SimpleNamespace(**dict(zip(names, refs, strict=True)))
    node = Node(pair)
    slab, feat, length, units = dims.slab, dims.feat, dims.length, dims.units
    width = dims.width
    model = 4 * feat
    hd = HEAD_DIM
    scale = HEAD_DIM ** (-0.5)
    tile = slab

    barrier = pltpu.get_barrier_semaphore()
    places = node.group() + [{"row": node.row(s)} for s in (1, 2, 3)]
    for where in places:
        pl.semaphore_signal(
            barrier, inc=1, device_id=where, device_id_type=pl.DeviceIdType.MESH
        )
    pl.semaphore_wait(barrier, len(places))

    background = []

    def tick():
        for steps in list(background):
            if next(steps, "over") == "over":
                background.remove(steps)

    def finish(steps):
        for _ in steps:
            pass
        if steps in background:
            background.remove(steps)

    def sems(name):
        return (getattr(k, name + "_send"), getattr(k, name + "_recv"))

    def run(steps):
        for _ in steps:
            tick()

    hidden = k.hidden[...]
    total = row_stat_steps(node, k.stat0, row_sums(hidden * hidden), sems("stat0"))
    rate_in = to_column(lax.rsqrt(total / model + epsilon))
    mine = span(node.c, slab)
    k.g_in[node.r, mine] = (hidden * rate_in * k.norm_in[...]).astype(LOW)
    steps = gather_steps(node, k.g_in, sems("ag_in"))
    next(steps)
    wa_steps = weight_steps(node, k.wa_src, k.wa, sems("wa"), k.own.at[0])
    next(wa_steps)
    background.append(wa_steps)
    k.g_cot[node.r, mine] = k.cot[...].astype(LOW)
    run(steps)
    finish(wa_steps)

    cot_steps = gather_steps(node, k.g_cot, sems("ag_cot"))
    next(cot_steps)
    w_steps = [
        weight_steps(node, k.wg_src, k.wg, sems("wg"), k.own.at[1]),
        weight_steps(node, k.wu_src, k.wu, sems("wu"), k.own.at[2]),
        weight_steps(node, k.wd_src, k.wd, sems("wd"), k.own.at[3]),
    ]
    for steps in w_steps:
        next(steps)

    for j in range(4):
        cols = pl.ds(j * tile, tile)
        acc = nt(k.wa[0, 0 : 3 * hd], k.g_in[0, cols])
        for i in (1, 2, 3):
            acc = acc + nt(k.wa[i, 0 : 3 * hd], k.g_in[i, cols])
        k.raw[:, cols] = acc
    raw_query, raw_key = k.raw[0:hd], k.raw[hd : 2 * hd]
    cos, sin = k.cos[...], k.sin[...]

    def rotated(raw, gain):
        rate = lax.rsqrt(jnp.mean(raw * raw, axis=0, keepdims=True) + epsilon)
        scaled = raw * rate * gain
        a, b = scaled[: hd // 2], scaled[hd // 2 :]
        return rate, jnp.concatenate([a * cos - b * sin, b * cos + a * sin], axis=0).astype(LOW)

    query_rate, query_turned = rotated(raw_query, k.query_gain[...])
    key_rate, key_turned = rotated(raw_key, k.key_gain[...])
    value_turned = k.raw[2 * hd :].astype(LOW)
    k.qt[...] = query_turned
    k.kt[...] = key_turned
    k.vt[...] = value_turned
    k.kn[...] = jnp.transpose(key_turned.astype(FLT)).astype(LOW)
    k.vn[...] = jnp.transpose(value_turned.astype(FLT)).astype(LOW)
    for j in range(4):
        cols = pl.ds(j * tile, tile)
        ext = (j + 1) * tile
        scores = nn(k.kn[0:ext], k.qt[:, cols]) * scale
        places = lax.broadcasted_iota(jnp.int32, (ext, tile), 0)
        own_place = lax.broadcasted_iota(jnp.int32, (ext, tile), 1) + j * tile
        allowed = (places >= k.start[0:1, cols]) & (places <= own_place)
        raised = jnp.where(allowed, jnp.exp(scores), 0.0)
        probs = raised * (1.0 / jnp.sum(raised, axis=0, keepdims=True))
        k.probs[0:ext, cols] = probs
        k.mixt[:, cols] = nn(k.vt[:, 0:ext], probs.astype(LOW))
    k.mix[...] = jnp.transpose(k.mixt[...]).astype(LOW)

    def out_part(r):
        def body(j, _):
            rows = span(j, tile)
            k.part[r, rows] = nn(k.mix[rows], k.wa[r, 3 * hd :]).astype(LOW)
            return 0

        lax.fori_loop(0, 4, body, 0)

    held = {}

    def take(name):
        def put(total):
            getattr(k, name)[...] = total

        return put

    def bufs(name, part, passed, out):
        return (part, getattr(k, name + "_got"), passed, getattr(k, name + "_far"), out, getattr(k, name + "_arr"))

    run(reduce_steps(node, bufs("ro", k.part, k.passed, k.leave), sems("ro"), out_part, take("blk")))
    resid = k.hidden[...] + k.blk[...]
    k.resid[...] = resid
    total = row_stat_steps(node, k.stat1, row_sums(resid * resid), sems("stat1"))
    rate_mid = to_column(lax.rsqrt(total / model + epsilon))
    k.rate_mid[...] = jnp.broadcast_to(rate_mid, k.rate_mid.shape)
    k.rate_in[...] = jnp.broadcast_to(rate_in, k.rate_in.shape)
    k.g_mid[node.r, mine] = (resid * rate_mid * k.norm_mid[...]).astype(LOW)
    background.append(cot_steps)
    for steps in w_steps:
        background.append(steps)

    def ff_in(r, i):
        def body(j, _):
            cols = span(j, tile)
            gate = nt(k.wg[r], k.g_mid[r, cols])
            up = nt(k.wu[r], k.g_mid[r, cols])
            if i:
                gate = gate + k.gate[:, cols]
                up = up + k.up[:, cols]
            k.gate[:, cols] = gate
            k.up[:, cols] = up
            return 0

        lax.fori_loop(0, 4, body, 0)

    def mid_done(r, i):
        if i == 0:
            for steps in [cot_steps] + w_steps:
                finish(steps)

            def body(j, _):
                cols = span(j, tile)
                acc = nt(k.wd[0], k.g_cot[0, cols])
                for i in (1, 2, 3):
                    acc = acc + nt(k.wd[i], k.g_cot[i, cols])
                k.gsw[:, cols] = acc
                return 0

            lax.fori_loop(0, 4, body, 0)
        ff_in(r, i)

    run(gather_steps(node, k.g_mid, sems("ag_mid"), mid_done))

    def activate(j, _):
        cols = span(j, tile)
        gate, up, gsw = k.gate[:, cols], k.up[:, cols], k.gsw[:, cols]
        sig = 1.0 / (1.0 + jnp.exp(-gate))
        act = gate * sig
        sw = act * up
        gga = gsw * up * sig * (1.0 + gate * (1.0 - sig))
        gua = gsw * act
        k.sw[:, cols] = sw.astype(LOW)
        k.gga[:, cols] = gga.astype(LOW)
        k.gua[:, cols] = gua.astype(LOW)
        k.sw_t[cols] = jnp.transpose(sw).astype(LOW)
        k.gga_t[cols] = jnp.transpose(gga).astype(LOW)
        k.gua_t[cols] = jnp.transpose(gua).astype(LOW)
        return 0

    lax.fori_loop(0, 4, activate, 0)

    def mid_part(r):
        def body(j, _):
            rows = span(j, tile)
            k.part[r, rows] = (nn(k.gga_t[rows], k.wg[r]) + nn(k.gua_t[rows], k.wu[r])).astype(LOW)
            return 0

        lax.fori_loop(0, 4, body, 0)

    def down_part(r):
        def body(j, _):
            rows = span(j, tile)
            k.part2[r, rows] = nn(k.sw_t[rows], k.wd[r]).astype(LOW)
            return 0

        lax.fori_loop(0, 4, body, 0)

    def outer(left, whole, target):
        def start():
            def body(i, _):
                target[i] = nn(left[...], whole[i]).astype(LOW)
                return 0

            lax.fori_loop(0, 4, body, 0)

        return start

    gd_steps = grad_steps(node, k.gs_d, k.yb_d, k.gr_d, k.od, sems("gd"), outer(k.sw, k.g_cot, k.gs_d))
    gg_steps = grad_steps(node, k.gs_g, k.yb_g, k.gr_g, k.og, sems("gg"), outer(k.gga, k.g_mid, k.gs_g))
    gu_steps = grad_steps(node, k.gs_u, k.yb_u, k.gr_u, k.ou, sems("gu"), outer(k.gua, k.g_mid, k.gs_u))
    steps = reduce_steps(node, bufs("rm", k.part, k.passed, k.leave), sems("rm"), mid_part, take("blk"))
    next(steps)
    next(gd_steps)
    next(steps)
    next(gg_steps)
    next(steps)
    next(gu_steps)
    next(steps)
    background += [gd_steps]
    run(steps)

    def put_output(total):
        k.output[...] = k.resid[...] + total

    down_steps = reduce_steps(node, bufs("rd", k.part2, k.passed2, k.leave2), sems("rd"), down_part, put_output)
    grad_normed_mid = k.blk[...]
    resid = k.resid[...]
    rate_mid = k.rate_mid[:, 0:1]
    scaled = k.norm_mid[...] * grad_normed_mid
    total = row_stat_steps(node, k.stat2, row_sums(scaled * resid), sems("stat2"))
    grad_resid = k.cot[...] + rate_mid * scaled - resid * (rate_mid * rate_mid * rate_mid * to_column(total / model))
    k.grad_resid[...] = grad_resid
    k.g_res[node.r, mine] = grad_resid.astype(LOW)
    steps = gather_steps(node, k.g_res, sems("ag_res"))
    next(steps)
    gain_mid = jnp.sum(grad_normed_mid * resid * rate_mid, axis=0, keepdims=True)
    background += [gg_steps, gu_steps, down_steps]
    run(steps)

    for j in range(4):
        cols = pl.ds(j * tile, tile)
        acc = nt(k.wa[0, 3 * hd :], k.g_res[0, cols])
        for i in (1, 2, 3):
            acc = acc + nt(k.wa[i, 3 * hd :], k.g_res[i, cols])
        k.gmt[:, cols] = acc.astype(LOW)
    k.dk[...] = jnp.zeros(k.dk.shape, FLT)
    k.dv[...] = jnp.zeros(k.dv.shape, FLT)
    for j in range(4):
        cols = pl.ds(j * tile, tile)
        ext = (j + 1) * tile
        probs = k.probs[0:ext, cols]
        k.dv[:, 0:ext] += nt(k.gmt[:, cols], probs.astype(LOW))
        grad_probs = nn(k.vn[0:ext], k.gmt[:, cols])
        inner = jnp.sum(probs * grad_probs, axis=0, keepdims=True)
        grad_scores = (probs * (grad_probs - inner) * scale).astype(LOW)
        k.dq[:, cols] = nn(k.kt[:, 0:ext], grad_scores)
        k.dk[:, 0:ext] += nt(k.qt[:, cols], grad_scores)
        tick()

    def turned_back(grad, raw, rate, gain):
        a, b = grad[: hd // 2], grad[hd // 2 :]
        t = jnp.concatenate([a * cos + b * sin, b * cos - a * sin], axis=0)
        scaled = gain * t
        inner = jnp.mean(scaled * raw, axis=0, keepdims=True)
        return (
            rate * scaled - raw * (rate * rate * rate * inner),
            jnp.sum(t * raw * rate, axis=1, keepdims=True),
        )

    cos, sin = k.cos[...], k.sin[...]
    raw_query, raw_key = k.raw[0:hd], k.raw[hd : 2 * hd]
    query_rate = lax.rsqrt(jnp.mean(raw_query * raw_query, axis=0, keepdims=True) + epsilon)
    key_rate = lax.rsqrt(jnp.mean(raw_key * raw_key, axis=0, keepdims=True) + epsilon)
    grad_query, gain_query = turned_back(k.dq[...], raw_query, query_rate, k.query_gain[...])
    grad_key, gain_key = turned_back(k.dk[...], raw_key, key_rate, k.key_gain[...])
    grad_proj = jnp.concatenate([grad_query, grad_key, k.dv[...]], axis=0)
    k.gp_turned[...] = grad_proj.astype(LOW)
    k.gp[...] = jnp.transpose(grad_proj).astype(LOW)

    k.gains[...] = jnp.zeros(k.gains.shape, FLT)
    k.gains[0:1, :] = gain_mid
    k.gains[1:2, 0:hd] = to_row(gain_query)
    k.gains[2:3, 0:hd] = to_row(gain_key)
    gain_copies = group_sum_start(node, k.gbox, k.gains[...], sems("gbox"))

    def in_part(r):
        def body(j, _):
            rows = span(j, tile)
            k.part[r, rows] = nn(k.gp[rows], k.wa[r, 0 : 3 * hd]).astype(LOW)
            return 0

        lax.fori_loop(0, 4, body, 0)

    def outer_attention():
        def body(i, _):
            k.gs_a[i, 0 : 3 * hd] = nn(k.gp_turned[...], k.g_in[i]).astype(LOW)
            k.gs_a[i, 3 * hd :] = nn(k.mixt[...].astype(LOW), k.g_res[i]).astype(LOW)
            return 0

        lax.fori_loop(0, 4, body, 0)

    ga_steps = grad_steps(node, k.gs_a, k.yb_a, k.gr_a, k.oa, sems("ga"), outer_attention)
    steps = reduce_steps(node, bufs("ri", k.part, k.passed, k.leave), sems("ri"), in_part, take("blk"))
    next(steps)
    next(steps)
    next(ga_steps)
    next(steps)
    background.append(ga_steps)
    run(steps)

    for copy in gain_copies:
        copy.wait_recv()
    gains = box_total(k.gbox)
    k.gains[...] = gains
    k.gain_mid[...] = gains
    k.qkbox[node.r] = gains
    qk_copies = [
        node.send(k.qkbox.at[node.r], k.qkbox.at[node.r], sems("qkbox"), s - 1, row=node.row(s))
        for s in (1, 2, 3)
    ]
    grad_normed_in = k.blk[...]
    rate_in = k.rate_in[:, 0:1]
    hidden = k.hidden[...]
    gain_in = jnp.sum(grad_normed_in * hidden * rate_in, axis=0, keepdims=True)
    in_copies = group_sum_start(
        node, k.inbox, jnp.broadcast_to(gain_in, k.gains.shape), sems("inbox")
    )
    scaled = k.norm_in[...] * grad_normed_in
    total = row_stat_steps(node, k.stat3, row_sums(scaled * hidden), sems("stat3"))
    k.grad_hidden[...] = (
        k.grad_resid[...] + rate_in * scaled - hidden * (rate_in * rate_in * rate_in * to_column(total / model))
    )
    for copy in qk_copies:
        copy.wait_recv()
    k.gain_qk[...] = box_total(k.qkbox)
    for copy in in_copies:
        copy.wait_recv()
    k.gain_in[...] = box_total(k.inbox)
    while background:
        tick()
    for copy in gain_copies + qk_copies + in_copies:
        copy.wait_send()


def doc_starts(documents):
    return jnp.sum((documents[None, :] < documents[:, None]).astype(jnp.int32), axis=1)


def local(
    hidden_in,
    segments,
    norm_in,
    w_query,
    w_key,
    w_value,
    query_gain,
    key_gain,
    w_out,
    norm_mid,
    w_gate,
    w_up,
    w_down,
    cotangent,
):
    rows, cols, dps = lax.axis_size("row"), lax.axis_size("col"), lax.axis_size("dp")
    pair = dps == 2
    slab, feat = hidden_in.shape
    length = segments.shape[1]
    hd = HEAD_DIM
    q_cols, k_cols = w_query.shape[1], w_key.shape[1]
    share = rows * hd // k_cols
    units = w_gate.shape[1] // rows
    assert rows == 4 and cols == 4 and q_cols == rows * hd and slab * cols == length
    dims = SimpleNamespace(slab=slab, feat=feat, length=length, units=units, width=4 * hd)

    starts = doc_starts(segments[0])
    positions = (jnp.arange(length, dtype=jnp.int32) - starts).astype(FLT)
    frequency = rope_base ** (-2.0 * jnp.arange(hd // 2, dtype=FLT) / hd)
    angles = frequency[:, None] * positions[None, :]
    cos, sin = jnp.cos(angles), jnp.sin(angles)
    query_turned, key_turned, value_turned = w_query.T, w_key.T, w_value.T
    wa_src = jnp.stack(
        [
            jnp.concatenate(
                [
                    query_turned[r * hd : (r + 1) * hd],
                    key_turned[(r // share) * hd : (r // share + 1) * hd],
                    value_turned[(r // share) * hd : (r // share + 1) * hd],
                    w_out[r * hd : (r + 1) * hd],
                ],
                axis=0,
            )
            for r in range(rows)
        ]
    )
    shape = jax.ShapeDtypeStruct
    ins = dict(
        hidden=hidden_in,
        cot=cotangent,
        norm_in=norm_in[None, :],
        norm_mid=norm_mid[None, :],
        query_gain=query_gain[:, None],
        key_gain=key_gain[:, None],
        cos=cos,
        sin=sin,
        start=jnp.broadcast_to(starts[None, :], (8, length)),
        wa_src=wa_src,
        wg_src=w_gate.T.reshape(rows, units, feat),
        wu_src=w_up.T.reshape(rows, units, feat),
        wd_src=w_down.reshape(rows, units, feat),
    )
    width = 4 * hd
    block = shape((slab, feat), FLT)
    outs = dict(
        output=block,
        grad_hidden=block,
        oa=shape((rows, width, feat), LOW),
        og=shape((rows, units, feat), LOW),
        ou=shape((rows, units, feat), LOW),
        od=shape((rows, units, feat), LOW),
        gain_mid=shape((8, feat), FLT),
        gain_qk=shape((8, feat), FLT),
        gain_in=shape((8, feat), FLT),
    )
    low = lambda *dims: pltpu.VMEM(dims, LOW)
    flt = lambda *dims: pltpu.VMEM(dims, FLT)
    group = cols * (2 if pair else 1)
    scratch = dict(
        resid=flt(slab, feat),
        grad_resid=flt(slab, feat),
        blk=flt(slab, feat),
        rate_in=flt(slab, 128),
        rate_mid=flt(slab, 128),
        wa=low(rows, width, feat),
        wg=low(rows, units, feat),
        wu=low(rows, units, feat),
        wd=low(rows, units, feat),
        part=low(rows, length, feat),
        part2=low(rows, length, feat),
        passed=low(rows, slab, feat),
        passed2=low(rows, slab, feat),
        leave=low(rows - 1, slab, feat),
        leave2=low(rows - 1, slab, feat),
        raw=flt(3 * hd, length),
        qt=low(hd, length),
        kt=low(hd, length),
        vt=low(hd, length),
        kn=low(length, hd),
        vn=low(length, hd),
        probs=flt(length, length),
        mixt=flt(hd, length),
        mix=low(length, hd),
        gmt=low(hd, length),
        dq=flt(hd, length),
        dk=flt(hd, length),
        dv=flt(hd, length),
        gp_turned=low(3 * hd, length),
        gp=low(length, 3 * hd),
        gate=flt(units, length),
        up=flt(units, length),
        gsw=flt(units, length),
        sw=low(units, length),
        gga=low(units, length),
        gua=low(units, length),
        sw_t=low(length, units),
        gga_t=low(length, units),
        gua_t=low(length, units),
        gains=flt(8, feat),
        gbox=flt(group, 8, feat),
        inbox=flt(group, 8, feat),
        qkbox=flt(rows, 8, feat),
        own=pltpu.SemaphoreType.DMA((4,)),
    )
    counts = dict(gbox=group - 1, inbox=group - 1, qkbox=3)
    for name in ("stat0", "stat1", "stat2", "stat3"):
        scratch[name] = flt(rows, 8, slab)
        counts[name] = 3
    for name in ("in", "cot", "mid", "res"):
        scratch["g_" + name] = low(rows, length, feat)
        counts["ag_" + name] = 15
    for name in ("ro", "rm", "rd", "ri"):
        scratch[name + "_got"] = low(rows, 2, slab, feat)
        scratch[name + "_far"] = low(rows, slab, feat)
        scratch[name + "_arr"] = low(rows - 1, slab, feat)
        counts[name] = 15
    for name, size in (("a", width), ("g", units), ("u", units), ("d", units)):
        half = size // 2 if pair else size
        scratch["gs_" + name] = low(rows, size, feat)
        scratch["yb_" + name] = low(rows, half, feat)
        scratch["gr_" + name] = low(rows, half, feat)
        counts["w" + name] = 6
        counts["g" + name] = 5
    for name, count in counts.items():
        scratch[name + "_send"] = pltpu.SemaphoreType.DMA((count,))
        scratch[name + "_recv"] = pltpu.SemaphoreType.DMA((count,))
    whole = pl.BlockSpec(memory_space=pltpu.VMEM)
    got = pl.pallas_call(
        functools.partial(kernel, dims, pair, tuple(ins) + tuple(outs) + tuple(scratch)),
        out_shape=tuple(outs.values()),
        in_specs=[whole] * len(ins),
        out_specs=(whole,) * len(outs),
        scratch_shapes=list(scratch.values()),
        compiler_params=pltpu.CompilerParams(
            collective_id=0, has_side_effects=True, vmem_limit_bytes=56 * 2**20
        ),
    )(*ins.values())
    o = SimpleNamespace(**dict(zip(outs, got, strict=True)))

    def over_dp(array):
        return array if pair else lax.psum(array, "dp")

    oa, og, ou, od = (over_dp(x).astype(FLT) for x in (o.oa, o.og, o.ou, o.od))
    gain_mid, gain_qk, gain_in = (over_dp(x[:3]) for x in (o.gain_mid, o.gain_qk, o.gain_in))

    def shared(part):
        return part.reshape(rows // share, share, hd, feat).sum(axis=1).reshape(k_cols, feat).T

    return (
        o.output,
        o.grad_hidden,
        gain_in[0],
        oa[:, 0:hd].reshape(q_cols, feat).T,
        shared(oa[:, hd : 2 * hd]),
        shared(oa[:, 2 * hd : 3 * hd]),
        gain_qk[1, :hd],
        gain_qk[2, :hd],
        oa[:, 3 * hd :].reshape(q_cols, feat),
        gain_mid[0],
        og.reshape(rows * units, feat).T,
        ou.reshape(rows * units, feat).T,
        od.reshape(rows * units, feat),
    )


def solution(mesh):
    stream = P(("dp", "col"), "row")
    first, last = P("row", "col"), P("col", "row")
    return jax.shard_map(
        local,
        mesh=mesh,
        in_specs=(stream, P("dp", None), P("row"), first, first, first, P(), P(), last, P("row"), first, first, last, stream),
        out_specs=(stream, stream, P("row"), first, first, first, P(), P(), last, P("row"), first, first, last),
        check_vma=False,
    )
```

```python
import functools
from types import SimpleNamespace

import jax
import jax.numpy as jnp
from jax import lax
from jax.experimental import pallas as pl
from jax.experimental.pallas import tpu as pltpu
from jax.sharding import PartitionSpec as P

HEAD_DIM = 64
epsilon = 1e-05
rope_base = 1000000.0
LOW = jnp.bfloat16
FLT = jnp.float32
ORDER = (1, 3, 2)


def nn(left_side, right_side):
    return jnp.dot(left_side, right_side, preferred_element_type=FLT)


def nt(left_side, right_side):
    return lax.dot_general(
        left_side, right_side, (((1,), (1,)), ((), ())), preferred_element_type=FLT
    )


def row_sums(block):
    return jnp.sum(jnp.transpose(block), axis=0, keepdims=True)


def to_column(row):
    return jnp.transpose(jnp.broadcast_to(row, (128, row.shape[1])))[:, :1]


def to_row(column):
    return jnp.transpose(jnp.broadcast_to(column, (column.shape[0], 128)))[:1, :]


class Node:
    def __init__(self, pair):
        self.pair = pair
        self.r = lax.axis_index("row")
        self.c = lax.axis_index("col")
        self.d = lax.axis_index("dp")
        self.near = self.c + 1 - 2 * lax.rem(self.c, 2)
        self.far = lax.rem(self.c + 2, 4)
        self.across = lax.rem(self.near + 2, 4)
        self.inner = lax.rem((self.r + 1) // 2, 2)
        self.inward = 1 + lax.rem(self.r, 2)
        self.outward = 3 * (self.r // 2)
        self.third = 3 - 3 * (self.r // 2)
        self.second = 2 - self.r // 2
        self.first = self.r + 1 - 2 * lax.rem(self.r, 2)

    def row(self, step):
        return lax.rem(self.r + step, 4)

    def send(self, src, dst, sems, slot, start=True, **where):
        copy = pltpu.make_async_remote_copy(
            src_ref=src,
            dst_ref=dst,
            send_sem=sems[0].at[slot[0] if isinstance(slot, tuple) else slot],
            recv_sem=sems[1].at[slot[1] if isinstance(slot, tuple) else slot],
            device_id=where,
            device_id_type=pl.DeviceIdType.MESH,
        )
        if start:
            copy.start()
        return copy

    def group(self):
        places = []
        for dp_step in range(2 if self.pair else 1):
            for col_step in range(4):
                if dp_step + col_step:
                    where = {"col": lax.rem(self.c + col_step, 4)}
                    if self.pair:
                        where["dp"] = lax.rem(self.d + dp_step, 2)
                    places.append(where)
        return places

    def group_slot(self):
        return self.d * 4 + self.c if self.pair else self.c


def span(block, size):
    return pl.ds(pl.multiple_of(block * size, size), size)


def gather_steps(node, whole, sems, done=None):
    size = whole.shape[1] // 4

    def here(r, c):
        return whole.at[r, span(c, size)]

    def along(slot, origin, to, start=True):
        block = here(origin, node.c)
        return node.send(block, block, sems, (slot, origin), start, row=to)

    def when_inner(slot, origin, to):
        @pl.when(node.inner == 1)
        def _():
            along(slot, origin, to)

    rows = [node.r, node.first, node.second, node.third]
    near, far, relay = {}, {}, {}

    def spread(i):
        block = here(rows[i], node.c)
        near[i] = node.send(block, block, sems, 5 + i, col=node.near)
        far[i] = node.send(block, block, sems, 9 + i, col=node.far)

    def pass_on(i):
        far[i].wait_recv()
        block = here(rows[i], node.far)
        relay[i] = node.send(block, block, sems, 13 + i, col=node.near)

    def complete(i):
        near[i].wait_recv()
        relay[i].wait_recv()
        if done is not None:
            done(rows[i], i)

    onward = {1: node.inward, 2: node.outward, 3: node.outward}
    own = along(0, node.r, node.inward)
    when_inner(1, node.r, node.outward)
    spread(0)
    yield
    for i in (1, 2, 3):
        along(0, rows[i], node.inward, start=False).wait_recv()
        when_inner(1 + i, rows[i], onward[i])
        spread(i)
        yield
        pass_on(i - 1)
        yield
        if i >= 2:
            complete(i - 2)
            yield
    pass_on(3)
    complete(2)
    yield
    complete(3)
    yield
    own.wait_send()

    @pl.when(node.inner == 1)
    def _():
        along(1, node.r, node.outward, start=False).wait_send()
        for i in (1, 2, 3):
            along(1 + i, rows[i], onward[i], start=False).wait_send()

    for copy in list(near.values()) + list(far.values()) + list(relay.values()):
        copy.wait_send()


def reduce_steps(node, bufs, sems, compute, finish):
    part, got, passed, from_far, out, arrived, carry = bufs
    size = part.shape[1] // 4
    rows = [node.third, node.second, node.first, node.r]
    first, second, crossing, along = {}, {}, {}, {}
    to = {0: node.inward, 1: node.inward, 2: node.inward + node.inner * (node.outward - node.inward)}
    slot_there = {0: 2 * node.inner, 1: 1 + 2 * node.inner, 2: 4 - node.inner}

    def begin(i):
        compute(rows[i])
        first[i] = node.send(
            part.at[rows[i], span(node.across, size)], got.at[i, 0], sems, i, col=node.near
        )
        second[i] = node.send(
            part.at[rows[i], span(node.near, size)], got.at[i, 1], sems, 4 + i, col=node.near
        )

    def cross(i):
        first[i].wait_recv()
        passed[i] = (
            part[rows[i], span(node.far, size)].astype(FLT) + got[i, 0].astype(FLT)
        ).astype(LOW)
        crossing[i] = node.send(passed.at[i], from_far.at[i], sems, 8 + i, col=node.far)

    def add_arrived(slot):
        node.send(
            out.at[0], arrived.at[slot], sems, (12, 12 + slot), False, row=node.inward
        ).wait_recv()
        carry[...] += arrived[slot].astype(FLT)

    def close(i):
        second[i].wait_recv()
        crossing[i].wait_recv()
        carry[...] = (
            part[rows[i], span(node.c, size)].astype(FLT)
            + got[i, 1].astype(FLT)
            + from_far[i].astype(FLT)
        )
        if i == 3:
            add_arrived(3)

        @pl.when(node.inner == 1)
        def _():
            add_arrived(4 if i == 3 else i)

        if i < 3:
            out[i] = carry[...].astype(LOW)
            along[i] = node.send(
                out.at[i], arrived.at[slot_there[i]], sems, (12 + i, 12 + slot_there[i]), row=to[i]
            )

    for i in range(4):
        begin(i)
        yield
        if i >= 1:
            cross(i - 1)
            yield
        if i >= 2:
            close(i - 2)
            yield
    cross(3)
    yield
    close(2)
    yield
    close(3)
    finish(carry[...])
    yield
    for group in (first, second, crossing, along):
        for copy in group.values():
            copy.wait_send()


def weight_steps(node, src, dst, sems):
    rows = dst.shape[1]
    half = rows // 2 if node.pair else rows
    offset = pl.multiple_of(node.d * half, half) if node.pair else 0
    mine = pl.ds(offset, half)
    along = {
        s: node.send(
            src.at[pl.ds(pl.multiple_of(node.row(s) * rows + offset, half), half)],
            dst.at[node.r, mine],
            sems,
            s - 1,
            row=node.row(s),
        )
        for s in ORDER
    }
    dst[node.r] = src[span(node.r, rows)]
    yield
    over = []
    for i, s in enumerate(ORDER):
        along[s].wait_recv()
        if node.pair:
            block = dst.at[lax.rem(node.r + 4 - s, 4), mine]
            over.append(node.send(block, block, sems, 3 + i, dp=1 - node.d))
        yield
    for copy in over:
        copy.wait_recv()
    yield
    for copy in list(along.values()) + over:
        copy.wait_send()


def grad_steps(node, src, partner, total, dst, sems, start, done):
    rows = src.shape[1]
    start()
    half = rows // 2 if node.pair else rows
    offset = pl.multiple_of(node.d * half, half) if node.pair else 0
    mine = pl.ds(offset, half)
    if node.pair:
        over = node.send(src.at[:, span(1 - node.d, half)], partner, sems, 0, dp=1 - node.d)
        yield
        over.wait_recv()
    else:
        yield

    def fill(i, _):
        value = src[i, mine]
        if node.pair:
            value = (value.astype(FLT) + partner[i].astype(FLT)).astype(LOW)
        total[i] = value
        return 0

    def place(r):
        return pl.ds(pl.multiple_of(r * rows + offset, half), half)

    back = []

    def send_back(r, i):
        if node.pair:
            block = dst.at[place(r)]
            back.append(node.send(block, block, sems, 4 + i, dp=1 - node.d))

    lax.fori_loop(0, 4, fill, 0)
    along = {
        s: node.send(total.at[node.row(s)], dst.at[place(node.r)], sems, s, row=node.row(s))
        for s in ORDER
    }
    dst[place(node.r)] = total[node.r]
    send_back(node.r, 0)
    yield
    for s in ORDER:
        along[s].wait_recv()
        send_back(lax.rem(node.r + 4 - s, 4), s)
    yield
    for copy in back:
        copy.wait_recv()
    done()
    yield
    for copy in list(along.values()) + back + ([over] if node.pair else []):
        copy.wait_send()


def row_stat_steps(node, box, sums, sems):
    box[node.r] = jnp.broadcast_to(sums, box.shape[1:])
    copies = [
        node.send(box.at[node.r], box.at[node.r], sems, s - 1, row=node.row(s)) for s in (1, 2, 3)
    ]
    for copy in copies:
        copy.wait_recv()
    total = box[0] + box[1] + box[2] + box[3]
    for copy in copies:
        copy.wait_send()
    return total[0:1]


def group_sum_start(node, box, value, sems):
    slot = node.group_slot()
    box[slot] = value
    return [
        node.send(box.at[slot], box.at[slot], sems, i, **where)
        for i, where in enumerate(node.group())
    ]


def box_total(box):
    total = box[0]
    for i in range(1, box.shape[0]):
        total = total + box[i]
    return total


def kernel(dims, pair, names, *refs):
    k = SimpleNamespace(**dict(zip(names, refs, strict=True)))
    node = Node(pair)
    slab, feat, length, units, share = dims.slab, dims.feat, dims.length, dims.units, dims.share
    rows_n = dims.rows
    model = rows_n * feat
    hd = HEAD_DIM
    width = 4 * hd
    scale = HEAD_DIM ** (-0.5)
    tile = slab

    loads = {}
    for i, name in enumerate(LOADED):
        copy = pltpu.make_async_copy(getattr(k, name), getattr(k, name + "_in"), k.loads.at[i])
        copy.start()
        loads[name] = copy
    stores = []

    def store(name):
        copy = pltpu.make_async_copy(
            getattr(k, "f_" + name), getattr(k, name), k.stores.at[len(stores)]
        )
        copy.start()
        stores.append(copy)

    barrier = pltpu.get_barrier_semaphore()
    places = node.group() + [{"row": node.row(s)} for s in (1, 2, 3)]
    for where in places:
        pl.semaphore_signal(
            barrier, inc=1, device_id=where, device_id_type=pl.DeviceIdType.MESH
        )
    loads["hidden"].wait()
    hidden = k.hidden_in[...]
    own_sums = row_sums(hidden * hidden)
    pl.semaphore_wait(barrier, len(places))

    every = []

    def begin(steps):
        every.append(steps)
        next(steps)
        return steps

    def finish(steps):
        for _ in steps:
            pass

    def adv(*many):
        for steps in many:
            next(steps, None)

    def sems(name):
        return (getattr(k, name + "_send"), getattr(k, name + "_recv"))

    def tiles(body):
        lax.fori_loop(0, length // tile, lambda j, _: body(j) or 0, 0)

    total = row_stat_steps(node, k.stat0, own_sums, sems("stat0"))
    rate_in = to_column(lax.rsqrt(total / model + epsilon))
    mine = span(node.c, slab)
    k.g_in[node.r, mine] = (hidden * rate_in * k.norm_in[...]).astype(LOW)
    main = begin(gather_steps(node, k.g_in, sems("ag_in")))

    for name in ("w_query", "w_key", "w_value", "w_out"):
        loads[name].wait()
    query_turned = jnp.transpose(k.w_query_in[...])
    key_turned = jnp.transpose(k.w_key_in[...])
    value_turned = jnp.transpose(k.w_value_in[...])
    for r in range(rows_n):
        at = r * width
        head = r // share
        k.wa_src[at : at + hd] = query_turned[r * hd : (r + 1) * hd]
        k.wa_src[at + hd : at + 2 * hd] = key_turned[head * hd : (head + 1) * hd]
        k.wa_src[at + 2 * hd : at + 3 * hd] = value_turned[head * hd : (head + 1) * hd]
        k.wa_src[at + 3 * hd : at + 4 * hd] = k.w_out_in[r * hd : (r + 1) * hd]
    wa_steps = begin(weight_steps(node, k.wa_src, k.wa, sems("wa")))

    loads["cot"].wait()
    k.g_cot[node.r, mine] = k.cot_in[...].astype(LOW)
    documents = k.segments[...].astype(FLT)
    document_column = jnp.transpose(jnp.broadcast_to(documents, (128, length)))[:, :1]
    starts = jnp.sum((document_column < documents).astype(FLT), axis=0, keepdims=True)
    k.start[...] = jnp.broadcast_to(starts, k.start.shape).astype(jnp.int32)
    positions = lax.broadcasted_iota(jnp.int32, (1, length), 1).astype(FLT) - starts
    angles = k.frequency[...] * positions
    k.cos[...] = jnp.cos(angles)
    k.sin[...] = jnp.sin(angles)
    loads["w_gate"].wait()
    loads["w_up"].wait()
    loads["w_down"].wait()
    for j in range(rows_n * units // 128):
        at = pl.ds(j * 128, 128)
        k.wg_src[at] = jnp.transpose(k.w_gate_in[:, at])
        k.wu_src[at] = jnp.transpose(k.w_up_in[:, at])

    query_gain = jnp.transpose(jnp.broadcast_to(k.query_gain[...], (128, hd)))[:, :1]
    key_gain = jnp.transpose(jnp.broadcast_to(k.key_gain[...], (128, hd)))[:, :1]
    adv(main, main)
    cot_steps = begin(gather_steps(node, k.g_cot, sems("ag_cot")))
    finish(main)
    finish(wa_steps)
    wg_steps = begin(weight_steps(node, k.wg_src, k.wg, sems("wg")))
    adv(cot_steps)
    def project(j):
        cols = span(j, tile)
        acc = nt(k.wa[0, 0 : 3 * hd], k.g_in[0, cols])
        for i in range(1, rows_n):
            acc = acc + nt(k.wa[i, 0 : 3 * hd], k.g_in[i, cols])
        k.raw[:, cols] = acc

    tiles(project)
    adv(cot_steps)
    raw_query, raw_key = k.raw[0:hd], k.raw[hd : 2 * hd]
    cos, sin = k.cos[...], k.sin[...]

    def rotated(raw, gain):
        rate = lax.rsqrt(jnp.mean(raw * raw, axis=0, keepdims=True) + epsilon)
        scaled = raw * rate * gain
        a, b = scaled[: hd // 2], scaled[hd // 2 :]
        return jnp.concatenate([a * cos - b * sin, b * cos + a * sin], axis=0)

    k.qt[...] = rotated(raw_query, query_gain).astype(LOW)
    key_turned = rotated(raw_key, key_gain)
    value_turned = k.raw[2 * hd :]
    k.kt[...] = key_turned.astype(LOW)
    k.vt[...] = value_turned.astype(LOW)
    k.kn[...] = jnp.transpose(key_turned).astype(LOW)
    k.vn[...] = jnp.transpose(value_turned).astype(LOW)
    for j in range(length // tile):
        cols = pl.ds(j * tile, tile)
        ext = (j + 1) * tile
        scores = nn(k.kn[0:ext], k.qt[:, cols]) * scale
        at = lax.broadcasted_iota(jnp.int32, (ext, tile), 0)
        own_place = lax.broadcasted_iota(jnp.int32, (ext, tile), 1) + j * tile
        allowed = (at >= k.start[0:1, cols]) & (at <= own_place)
        raised = jnp.where(allowed, jnp.exp(scores), 0.0)
        probs = raised * (1.0 / jnp.sum(raised, axis=0, keepdims=True))
        k.probs[0:ext, cols] = probs
        k.mixt[:, cols] = nn(k.vt[:, 0:ext], probs.astype(LOW))
        adv(cot_steps)
    k.mix[...] = jnp.transpose(k.mixt[...]).astype(LOW)
    def out_part(r):
        def body(j):
            rows = span(j, tile)
            k.part[r, rows] = nn(k.mix[rows], k.wa[r, 3 * hd :]).astype(LOW)

        tiles(body)

    def take(total):
        k.blk[...] = total

    def bufs(name, second=""):
        return (
            getattr(k, "part" + second),
            getattr(k, name + "_got"),
            getattr(k, "passed" + second),
            getattr(k, name + "_far"),
            getattr(k, "leave" + second),
            getattr(k, name + "_arr"),
            getattr(k, "carry" + second),
        )

    main = begin(reduce_steps(node, bufs("ro"), sems("ro"), out_part, take))
    wu_steps = begin(weight_steps(node, k.wu_src, k.wu, sems("wu")))
    adv(main, main)
    adv(cot_steps)
    adv(main, main)
    adv(cot_steps)
    adv(main, main)
    adv(cot_steps)
    wd_steps = begin(weight_steps(node, k.w_down_in, k.wd, sems("wd")))
    finish(main)
    resid = k.hidden_in[...] + k.blk[...]
    k.resid[...] = resid
    total = row_stat_steps(node, k.stat1, row_sums(resid * resid), sems("stat1"))
    rate_mid = to_column(lax.rsqrt(total / model + epsilon))
    k.rate_mid[...] = jnp.broadcast_to(rate_mid, k.rate_mid.shape)
    k.rate_in[...] = jnp.broadcast_to(rate_in, k.rate_in.shape)
    k.g_mid[node.r, mine] = (resid * rate_mid * k.norm_mid[...]).astype(LOW)
    def ff_in(r, i):
        def body(j):
            cols = span(j, tile)
            gate = nt(k.wg[r], k.g_mid[r, cols])
            up = nt(k.wu[r], k.g_mid[r, cols])
            if i:
                gate = gate + k.gate[:, cols]
                up = up + k.up[:, cols]
            k.gate[:, cols] = gate
            k.up[:, cols] = up

        tiles(body)

    def mid_done(r, i):
        if i == 0:
            finish(wg_steps)
            finish(wu_steps)
        if i == 2:
            finish(wd_steps)
            finish(cot_steps)

            def body(j):
                cols = span(j, tile)
                acc = nt(k.wd[0], k.g_cot[0, cols])
                for i in range(1, rows_n):
                    acc = acc + nt(k.wd[i], k.g_cot[i, cols])
                k.gsw[:, cols] = acc

            tiles(body)
        ff_in(r, i)

    main = begin(gather_steps(node, k.g_mid, sems("ag_mid"), mid_done))
    adv(wg_steps, wg_steps, wg_steps, cot_steps)
    adv(main)
    adv(wu_steps, wu_steps, wu_steps, cot_steps)
    adv(main, main)
    adv(wd_steps, wd_steps, wd_steps, cot_steps)
    finish(main)
    def activate(j):
        cols = span(j, tile)
        gate, up, gsw = k.gate[:, cols], k.up[:, cols], k.gsw[:, cols]
        sig = 1.0 / (1.0 + jnp.exp(-gate))
        act = gate * sig
        sw = act * up
        gga = gsw * up * sig * (1.0 + gate * (1.0 - sig))
        gua = gsw * act
        k.sw[:, cols] = sw.astype(LOW)
        k.gga[:, cols] = gga.astype(LOW)
        k.gua[:, cols] = gua.astype(LOW)
        k.sw_t[cols] = jnp.transpose(sw).astype(LOW)
        k.gga_t[cols] = jnp.transpose(gga).astype(LOW)
        k.gua_t[cols] = jnp.transpose(gua).astype(LOW)

    tiles(activate)
    def mid_part(r):
        def body(j):
            rows = span(j, tile)
            k.part[r, rows] = (nn(k.gga_t[rows], k.wg[r]) + nn(k.gua_t[rows], k.wu[r])).astype(LOW)

        tiles(body)

    def down_part(r):
        def body(j):
            rows = span(j, tile)
            k.part2[r, rows] = nn(k.sw_t[rows], k.wd[r]).astype(LOW)

        tiles(body)

    def outer(left, whole, target):
        def start():
            def body(i, _):
                target[i] = nn(left[...], whole[i]).astype(LOW)
                return 0

            lax.fori_loop(0, rows_n, body, 0)

        return start

    def turned_out(source, target, name):
        def done():
            for j in range(rows_n * units // 128):
                at = pl.ds(j * 128, 128)
                target[:, at] = jnp.transpose(source[at].astype(FLT))
            store(name)

        return done

    def down_out():
        k.f_grad_down[...] = k.od[...].astype(FLT)
        store("grad_down")

    gd_steps = grad_steps(
        node, k.gs_d, k.yb_d, k.gr_d, k.od, sems("gd"), outer(k.sw, k.g_cot, k.gs_d), down_out
    )
    gg_steps = grad_steps(
        node, k.gs_g, k.yb_g, k.gr_g, k.og, sems("gg"), outer(k.gga, k.g_mid, k.gs_g),
        turned_out(k.og, k.f_grad_gate, "grad_gate"),
    )
    gu_steps = grad_steps(
        node, k.gs_u, k.yb_u, k.gr_u, k.ou, sems("gu"), outer(k.gua, k.g_mid, k.gs_u),
        turned_out(k.ou, k.f_grad_up, "grad_up"),
    )

    def put_output(total):
        k.f_output[...] = k.resid[...] + total
        store("output")

    main = begin(reduce_steps(node, bufs("rm"), sems("rm"), mid_part, take))
    begin(gd_steps)
    adv(main, main)
    begin(gg_steps)
    adv(main, main)
    begin(gu_steps)
    adv(main, main)
    adv(gd_steps)
    finish(main)
    down_steps = reduce_steps(node, bufs("rd", "2"), sems("rd"), down_part, put_output)
    grad_normed_mid = k.blk[...]
    resid = k.resid[...]
    rate_mid = k.rate_mid[:, 0:1]
    scaled = k.norm_mid[...] * grad_normed_mid
    total = row_stat_steps(node, k.stat2, row_sums(scaled * resid), sems("stat2"))
    grad_resid = k.cot_in[...] + rate_mid * scaled - resid * (
        rate_mid * rate_mid * rate_mid * to_column(total / model)
    )
    k.grad_resid[...] = grad_resid
    k.g_res[node.r, mine] = grad_resid.astype(LOW)
    main = begin(gather_steps(node, k.g_res, sems("ag_res")))
    begin(down_steps)
    gain_mid = jnp.sum(grad_normed_mid * resid * rate_mid, axis=0, keepdims=True)
    adv(main)
    adv(gg_steps)
    adv(down_steps, down_steps)
    adv(main, main)
    adv(gd_steps, gu_steps)
    adv(down_steps, down_steps)
    adv(main, main, main)
    adv(gg_steps)
    finish(main)
    def grad_mixed(j):
        cols = span(j, tile)
        acc = nt(k.wa[0, 3 * hd :], k.g_res[0, cols])
        for i in range(1, rows_n):
            acc = acc + nt(k.wa[i, 3 * hd :], k.g_res[i, cols])
        k.gmt[:, cols] = acc.astype(LOW)

    tiles(grad_mixed)
    k.dk[...] = jnp.zeros(k.dk.shape, FLT)
    k.dv[...] = jnp.zeros(k.dv.shape, FLT)
    for j in range(length // tile):
        cols = pl.ds(j * tile, tile)
        ext = (j + 1) * tile
        probs = k.probs[0:ext, cols]
        k.dv[:, 0:ext] += nt(k.gmt[:, cols], probs.astype(LOW))
        grad_probs = nn(k.vn[0:ext], k.gmt[:, cols])
        inner = jnp.sum(probs * grad_probs, axis=0, keepdims=True)
        grad_scores = (probs * (grad_probs - inner) * scale).astype(LOW)
        k.dq[:, cols] = nn(k.kt[:, 0:ext], grad_scores)
        k.dk[:, 0:ext] += nt(k.qt[:, cols], grad_scores)
        adv(down_steps)

    def turned_back(grad, raw, gain):
        rate = lax.rsqrt(jnp.mean(raw * raw, axis=0, keepdims=True) + epsilon)
        a, b = grad[: hd // 2], grad[hd // 2 :]
        t = jnp.concatenate([a * cos + b * sin, b * cos - a * sin], axis=0)
        scaled = gain * t
        inner = jnp.mean(scaled * raw, axis=0, keepdims=True)
        return (
            rate * scaled - raw * (rate * rate * rate * inner),
            jnp.sum(t * raw * rate, axis=1, keepdims=True),
        )

    cos, sin = k.cos[...], k.sin[...]
    grad_query, gain_query = turned_back(k.dq[...], k.raw[0:hd], query_gain)
    grad_key, gain_key = turned_back(k.dk[...], k.raw[hd : 2 * hd], key_gain)
    grad_proj = jnp.concatenate([grad_query, grad_key, k.dv[...]], axis=0)
    k.gp_turned[...] = grad_proj.astype(LOW)
    k.gp[...] = jnp.transpose(grad_proj).astype(LOW)
    def in_part(r):
        def body(j):
            rows = span(j, tile)
            k.part[r, rows] = nn(k.gp[rows], k.wa[r, 0 : 3 * hd]).astype(LOW)

        tiles(body)

    def outer_attention():
        def body(i, _):
            k.gs_a[i, 0 : 3 * hd] = nn(k.gp_turned[...], k.g_in[i]).astype(LOW)
            k.gs_a[i, 3 * hd :] = nn(k.mixt[...].astype(LOW), k.g_res[i]).astype(LOW)
            return 0

        lax.fori_loop(0, rows_n, body, 0)

    def attention_out():
        def part(r, i):
            return k.oa[r * width + i * hd : r * width + (i + 1) * hd].astype(FLT)

        k.f_grad_query[...] = jnp.transpose(
            jnp.concatenate([part(r, 0) for r in range(rows_n)], axis=0)
        )
        for i, target in ((1, k.f_grad_key), (2, k.f_grad_value)):
            heads = []
            for h in range(rows_n // share):
                acc = part(h * share, i)
                for r in range(h * share + 1, (h + 1) * share):
                    acc = acc + part(r, i)
                heads.append(acc)
            target[...] = jnp.transpose(jnp.concatenate(heads, axis=0))
        for r in range(rows_n):
            k.f_grad_out[r * hd : (r + 1) * hd] = part(r, 3)
        for name in ("grad_query", "grad_key", "grad_value", "grad_out"):
            store(name)

    ga_steps = grad_steps(
        node, k.gs_a, k.yb_a, k.gr_a, k.oa, sems("ga"), outer_attention, attention_out
    )
    main = begin(reduce_steps(node, bufs("ri"), sems("ri"), in_part, take))
    k.gains[...] = jnp.zeros(k.gains.shape, FLT)
    k.gains[0:1, :] = gain_mid
    k.gains[1:2, 0:hd] = to_row(gain_query)
    k.gains[2:3, 0:hd] = to_row(gain_key)
    gain_copies = group_sum_start(node, k.gbox, k.gains[...], sems("gbox"))
    begin(ga_steps)
    adv(main, main)
    adv(gu_steps)
    adv(main, main)
    adv(ga_steps)
    adv(main, main, main)
    adv(gd_steps, gg_steps, gu_steps)
    finish(main)
    adv(ga_steps)
    grad_normed_in = k.blk[...]
    rate_in = k.rate_in[:, 0:1]
    hidden = k.hidden_in[...]
    gain_in = jnp.sum(grad_normed_in * hidden * rate_in, axis=0, keepdims=True)
    in_copies = group_sum_start(
        node, k.inbox, jnp.broadcast_to(gain_in, k.gains.shape), sems("inbox")
    )
    for copy in gain_copies:
        copy.wait_recv()
    gains = box_total(k.gbox)
    k.gain_mid[...] = gains[0:1]
    k.qkbox[node.r] = gains
    qk_copies = [
        node.send(k.qkbox.at[node.r], k.qkbox.at[node.r], sems("qkbox"), s - 1, row=node.row(s))
        for s in (1, 2, 3)
    ]
    scaled = k.norm_in[...] * grad_normed_in
    total = row_stat_steps(node, k.stat3, row_sums(scaled * hidden), sems("stat3"))
    k.f_grad_hidden[...] = (
        k.grad_resid[...] + rate_in * scaled - hidden * (rate_in * rate_in * rate_in * to_column(total / model))
    )
    store("grad_hidden")
    finish(down_steps)
    for steps in (gd_steps, gg_steps, gu_steps, ga_steps):
        finish(steps)
    for copy in qk_copies:
        copy.wait_recv()
    gains = box_total(k.qkbox)
    k.gain_query[...] = gains[1:2, 0:hd]
    k.gain_key[...] = gains[2:3, 0:hd]
    for copy in in_copies:
        copy.wait_recv()
    k.gain_in[...] = box_total(k.inbox)[0:1]
    for copy in gain_copies + qk_copies + in_copies:
        copy.wait_send()
    for copy in stores:
        copy.wait()


def copy_kernel(count, *refs):
    held, arrive, leave = refs[2 * count : 3 * count], refs[-2], refs[-1]
    inward = [pltpu.make_async_copy(refs[i], held[i], arrive.at[i]) for i in range(count)]
    outward = [
        pltpu.make_async_copy(held[i], refs[count + i], leave.at[i]) for i in range(count)
    ]
    for copy in inward:
        copy.start()
    for came, left in zip(inward, outward):
        came.wait()
        left.start()
    for copy in outward:
        copy.wait()


LOADED = ("hidden", "w_query", "w_key", "w_value", "w_out", "cot", "w_gate", "w_up", "w_down")


def local(
    hidden_in,
    segments,
    norm_in,
    w_query,
    w_key,
    w_value,
    query_gain,
    key_gain,
    w_out,
    norm_mid,
    w_gate,
    w_up,
    w_down,
    cotangent,
):
    rows, cols, dps = lax.axis_size("row"), lax.axis_size("col"), lax.axis_size("dp")
    pair = dps == 2
    slab, feat = hidden_in.shape
    length = segments.shape[1]
    hd = HEAD_DIM
    q_cols, k_cols, u_cols = w_query.shape[1], w_key.shape[1], w_gate.shape[1]
    share = rows * hd // k_cols
    units = u_cols // rows
    assert rows == 4 and cols == 4 and q_cols == rows * hd and slab * cols == length
    dims = SimpleNamespace(
        slab=slab, feat=feat, length=length, units=units, share=share, rows=rows
    )
    frequency = rope_base ** (-2.0 * jnp.arange(hd // 2, dtype=FLT) / hd)
    shape = jax.ShapeDtypeStruct
    small = dict(
        segments=segments,
        norm_in=norm_in[None, :],
        norm_mid=norm_mid[None, :],
        query_gain=query_gain[None, :],
        key_gain=key_gain[None, :],
        frequency=jnp.broadcast_to(frequency[:, None], (hd // 2, 128))[:, :1],
    )
    large = dict(
        hidden=hidden_in,
        cot=cotangent,
        w_query=w_query,
        w_key=w_key,
        w_value=w_value,
        w_out=w_out,
        w_gate=w_gate,
        w_up=w_up,
        w_down=w_down,
    )
    block = (slab, feat)
    large_outs = dict(
        output=block,
        grad_hidden=block,
        grad_query=w_query.shape,
        grad_key=w_key.shape,
        grad_value=w_value.shape,
        grad_out=w_out.shape,
        grad_gate=w_gate.shape,
        grad_up=w_up.shape,
        grad_down=w_down.shape,
    )
    small_outs = dict(
        gain_mid=(1, feat), gain_in=(1, feat), gain_query=(1, hd), gain_key=(1, hd)
    )
    width = 4 * hd
    low = lambda *dims: pltpu.VMEM(dims, LOW)
    flt = lambda *dims: pltpu.VMEM(dims, FLT)
    group = cols * (2 if pair else 1)
    scratch = {name + "_in": pltpu.VMEM(array.shape, array.dtype) for name, array in large.items()}
    scratch.update({"f_" + name: flt(*dims) for name, dims in large_outs.items()})
    scratch.update(
        loads=pltpu.SemaphoreType.DMA((len(large),)),
        stores=pltpu.SemaphoreType.DMA((len(large_outs),)),
        wa_src=low(rows * width, feat),
        wg_src=low(rows * units, feat),
        wu_src=low(rows * units, feat),
        resid=flt(slab, feat),
        grad_resid=flt(slab, feat),
        blk=flt(slab, feat),
        carry=flt(slab, feat),
        carry2=flt(slab, feat),
        rate_in=flt(slab, 128),
        rate_mid=flt(slab, 128),
        start=pltpu.VMEM((8, length), jnp.int32),
        cos=flt(hd // 2, length),
        sin=flt(hd // 2, length),
        wa=low(rows, width, feat),
        wg=low(rows, units, feat),
        wu=low(rows, units, feat),
        wd=low(rows, units, feat),
        part=low(rows, length, feat),
        part2=low(rows, length, feat),
        passed=low(rows, slab, feat),
        passed2=low(rows, slab, feat),
        leave=low(rows - 1, slab, feat),
        leave2=low(rows - 1, slab, feat),
        raw=flt(3 * hd, length),
        qt=low(hd, length),
        kt=low(hd, length),
        vt=low(hd, length),
        kn=low(length, hd),
        vn=low(length, hd),
        probs=flt(length, length),
        mixt=flt(hd, length),
        mix=low(length, hd),
        gmt=low(hd, length),
        dq=flt(hd, length),
        dk=flt(hd, length),
        dv=flt(hd, length),
        gp_turned=low(3 * hd, length),
        gp=low(length, 3 * hd),
        gate=flt(units, length),
        up=flt(units, length),
        gsw=flt(units, length),
        sw=low(units, length),
        gga=low(units, length),
        gua=low(units, length),
        sw_t=low(length, units),
        gga_t=low(length, units),
        gua_t=low(length, units),
        gains=flt(8, feat),
        gbox=flt(group, 8, feat),
        inbox=flt(group, 8, feat),
        qkbox=flt(rows, 8, feat),
    )
    counts = dict(gbox=group - 1, inbox=group - 1, qkbox=3)
    for name in ("stat0", "stat1", "stat2", "stat3"):
        scratch[name] = flt(rows, 8, slab)
        counts[name] = 3
    for name in ("in", "cot", "mid", "res"):
        scratch["g_" + name] = low(rows, length, feat)
        counts["ag_" + name] = 17
    for name in ("ro", "rm", "rd", "ri"):
        scratch[name + "_got"] = low(rows, 2, slab, feat)
        scratch[name + "_far"] = low(rows, slab, feat)
        scratch[name + "_arr"] = low(rows + 1, slab, feat)
        counts[name] = 17
    for name, size in (("a", width), ("g", units), ("u", units), ("d", units)):
        half = size // 2 if pair else size
        scratch["gs_" + name] = low(rows, size, feat)
        scratch["yb_" + name] = low(rows, half, feat)
        scratch["gr_" + name] = low(rows, half, feat)
        scratch["o" + name] = low(rows * size, feat)
        counts["w" + name] = 6
        counts["g" + name] = 8
    for name, count in counts.items():
        scratch[name + "_send"] = pltpu.SemaphoreType.DMA((count,))
        scratch[name + "_recv"] = pltpu.SemaphoreType.DMA((count,))
    vmem, anywhere = pl.BlockSpec(memory_space=pltpu.VMEM), pl.BlockSpec(memory_space=pl.ANY)
    names = tuple(small) + tuple(large) + tuple(small_outs) + tuple(large_outs) + tuple(scratch)
    out_shape = tuple(shape(d, FLT) for d in (small_outs | large_outs).values())
    got = pl.pallas_call(
        functools.partial(kernel, dims, pair, names),
        out_shape=out_shape,
        in_specs=[vmem] * len(small) + [anywhere] * len(large),
        out_specs=(vmem,) * len(small_outs) + (anywhere,) * len(large_outs),
        scratch_shapes=list(scratch.values()),
        compiler_params=pltpu.CompilerParams(
            collective_id=0, has_side_effects=True, vmem_limit_bytes=60 * 2**20
        ),
    )(*small.values(), *large.values())
    if pair:
        got = pl.pallas_call(
            functools.partial(copy_kernel, len(got)),
            out_shape=out_shape,
            in_specs=[anywhere] * len(got),
            out_specs=(anywhere,) * len(got),
            scratch_shapes=[pltpu.VMEM(array.shape, array.dtype) for array in got]
            + [pltpu.SemaphoreType.DMA((len(got),))] * 2,
        )(*got)
    o = SimpleNamespace(**dict(zip(tuple(small_outs) + tuple(large_outs), got, strict=True)))
    if not pair:
        for name in tuple(small_outs) + tuple(large_outs)[2:]:
            setattr(o, name, lax.psum(getattr(o, name), "dp"))
    return (
        o.output,
        o.grad_hidden,
        o.gain_in[0],
        o.grad_query,
        o.grad_key,
        o.grad_value,
        o.gain_query[0],
        o.gain_key[0],
        o.grad_out,
        o.gain_mid[0],
        o.grad_gate,
        o.grad_up,
        o.grad_down,
    )


def solution(mesh):
    stream = P(("dp", "col"), "row")
    first, last = P("row", "col"), P("col", "row")
    return jax.shard_map(
        local,
        mesh=mesh,
        in_specs=(stream, P("dp", None), P("row"), first, first, first, P(), P(), last, P("row"), first, first, last, stream),
        out_specs=(stream, stream, P("row"), first, first, first, P(), P(), last, P("row"), first, first, last),
        check_vma=False,
    )
```

```python
import functools
from types import SimpleNamespace

import jax
import jax.numpy as jnp
import numpy as np
from jax import lax
from jax.experimental import pallas as pl
from jax.experimental.pallas import tpu as pltpu
from jax.sharding import PartitionSpec as P

HEAD_DIM = 64
epsilon = 1e-05
rope_base = 1000000.0
LOW = jnp.bfloat16
FLT = jnp.float32
ORDER = (1, 3, 2)


def nn(left_side, right_side):
    return jnp.dot(left_side, right_side, preferred_element_type=FLT)


def nt(left_side, right_side):
    return lax.dot_general(
        left_side, right_side, (((1,), (1,)), ((), ())), preferred_element_type=FLT
    )


def row_sums(block):
    return jnp.sum(jnp.transpose(block), axis=0, keepdims=True)


def to_column(row):
    return jnp.transpose(jnp.broadcast_to(row, (128, row.shape[1])))[:, :1]


def to_row(column):
    return jnp.transpose(jnp.broadcast_to(column, (column.shape[0], 128)))[:1, :]


class Node:
    def __init__(self, pair):
        self.pair = pair
        self.r = lax.axis_index("row")
        self.c = lax.axis_index("col")
        self.d = lax.axis_index("dp")
        self.near = self.c + 1 - 2 * lax.rem(self.c, 2)
        self.far = lax.rem(self.c + 2, 4)
        self.across = lax.rem(self.near + 2, 4)
        self.inner = lax.rem((self.r + 1) // 2, 2)
        self.inward = 1 + lax.rem(self.r, 2)
        self.outward = 3 * (self.r // 2)
        self.third = 3 - 3 * (self.r // 2)
        self.second = 2 - self.r // 2
        self.first = self.r + 1 - 2 * lax.rem(self.r, 2)

    def row(self, step):
        return lax.rem(self.r + step, 4)

    def send(self, src, dst, sems, slot, start=True, **where):
        copy = pltpu.make_async_remote_copy(
            src_ref=src,
            dst_ref=dst,
            send_sem=sems[0].at[slot[0] if isinstance(slot, tuple) else slot],
            recv_sem=sems[1].at[slot[1] if isinstance(slot, tuple) else slot],
            device_id=where,
            device_id_type=pl.DeviceIdType.MESH,
        )
        if start:
            copy.start()
        return copy

    def group(self):
        places = []
        for dp_step in range(2 if self.pair else 1):
            for col_step in range(4):
                if dp_step + col_step:
                    where = {"col": lax.rem(self.c + col_step, 4)}
                    if self.pair:
                        where["dp"] = lax.rem(self.d + dp_step, 2)
                    places.append(where)
        return places

    def group_slot(self):
        return self.d * 4 + self.c if self.pair else self.c


def span(block, size):
    return pl.ds(pl.multiple_of(block * size, size), size)


def gather_steps(node, whole, sems, pieces, lag, done=None):
    size = whole.shape[1] // 4
    cut = size // pieces

    def here(r, c, h):
        return whole.at[r, pl.ds(pl.multiple_of(c * size + h * cut, cut), cut)]

    def along(slot, origin, h, to, start=True):
        block = here(origin, node.c, h)
        return node.send(
            block, block, sems, (slot * pieces + h, origin * pieces + h), start, row=to
        )

    def when_inner(slot, origin, h, to):
        @pl.when(node.inner == 1)
        def _():
            along(slot, origin, h, to)

    rows = [node.r, node.first, node.second, node.third]
    near, far, relay = {}, {}, {}
    waiting = []

    def spread(i, h):
        block = here(rows[i], node.c, h)
        far[i, h] = node.send(block, block, sems, 9 * pieces + i * pieces + h, col=node.far)
        near[i, h] = node.send(block, block, sems, 5 * pieces + i * pieces + h, col=node.near)
        waiting.append((i, h))

    def pass_on():
        i, h = waiting.pop(0)
        far[i, h].wait_recv()
        block = here(rows[i], node.far, h)
        relay[i, h] = node.send(block, block, sems, 13 * pieces + i * pieces + h, col=node.near)

    def complete(i):
        for h in range(pieces):
            near[i, h].wait_recv()
            relay[i, h].wait_recv()
        if done is not None:
            done(rows[i], i)

    onward = {1: node.inward, 2: node.outward, 3: node.outward}
    own = []
    for h in range(pieces):
        own.append(along(0, node.r, h, node.inward))
        when_inner(1, node.r, h, node.outward)
        spread(0, h)
    yield
    for i in (1, 2, 3):
        for h in range(pieces):
            along(0, rows[i], h, node.inward, start=False).wait_recv()
            when_inner(1 + i, rows[i], h, onward[i])
            spread(i, h)
            while len(waiting) > lag:
                pass_on()
            yield
        if i >= 2:
            while waiting[0][0] <= i - 2:
                pass_on()
            complete(i - 2)
            yield
    for i in (2, 3):
        while waiting and waiting[0][0] <= i:
            pass_on()
        complete(i)
        yield
    for copy in own:
        copy.wait_send()

    @pl.when(node.inner == 1)
    def _():
        for h in range(pieces):
            along(1, node.r, h, node.outward, start=False).wait_send()
            for i in (1, 2, 3):
                along(1 + i, rows[i], h, onward[i], start=False).wait_send()

    for copy in list(near.values()) + list(far.values()) + list(relay.values()):
        copy.wait_send()


def reduce_steps(node, bufs, sems, pieces, compute, finish):
    part, got, passed, from_far, out, arrived, carry = bufs
    size = part.shape[1] // 4
    cut = size // pieces
    rows = [node.third, node.second, node.first, node.r]
    first, second, crossing, along = {}, {}, {}, {}
    to = {0: node.inward, 1: node.inward, 2: node.inward + node.inner * (node.outward - node.inward)}
    slot_there = {0: 2 * node.inner, 1: 1 + 2 * node.inner, 2: 4 - node.inner}

    def piece(c, h):
        return pl.ds(pl.multiple_of(c * size + h * cut, cut), cut)

    def begin(i):
        compute(rows[i])
        for h in range(pieces):
            first[i, h] = node.send(
                part.at[rows[i], piece(node.across, h)],
                got.at[i, 0, pl.ds(h * cut, cut)],
                sems,
                i * pieces + h,
                col=node.near,
            )
        second[i] = node.send(
            part.at[rows[i], span(node.near, size)], got.at[i, 1], sems, 4 * pieces + i, col=node.near
        )

    def cross(i):
        for h in range(pieces):
            at = pl.ds(h * cut, cut)
            first[i, h].wait_recv()
            passed[i, at] = (
                part[rows[i], piece(node.far, h)].astype(FLT) + got[i, 0, at].astype(FLT)
            ).astype(LOW)
            crossing[i, h] = node.send(
                passed.at[i, at],
                from_far.at[i, at],
                sems,
                4 * pieces + 4 + i * pieces + h,
                col=node.far,
            )

    base = 8 * pieces + 4

    def add_arrived(slot, h):
        at = pl.ds(h * cut, cut)
        node.send(
            out.at[0, at],
            arrived.at[slot, at],
            sems,
            (base, base + slot * pieces + h),
            False,
            row=node.inward,
        ).wait_recv()
        carry[at] += arrived[slot, at].astype(FLT)

    def close(i, h):
        at = pl.ds(h * cut, cut)
        if h == 0:
            second[i].wait_recv()
        crossing[i, h].wait_recv()
        carry[at] = (
            part[rows[i], piece(node.c, h)].astype(FLT)
            + got[i, 1, at].astype(FLT)
            + from_far[i, at].astype(FLT)
        )
        if i == 3:
            add_arrived(3, h)

        @pl.when(node.inner == 1)
        def _():
            add_arrived(4 if i == 3 else i, h)

        if i < 3:
            out[i, at] = carry[at].astype(LOW)
            along[i, h] = node.send(
                out.at[i, at],
                arrived.at[slot_there[i], at],
                sems,
                (base + i * pieces + h, base + slot_there[i] * pieces + h),
                row=to[i],
            )

    for i in range(4):
        begin(i)
        yield
        if i >= 1:
            cross(i - 1)
            yield
    cross(3)
    yield
    for i in range(4):
        for h in range(pieces):
            close(i, h)
            yield
    finish(carry[...])
    yield
    for group in (first, second, crossing, along):
        for copy in group.values():
            copy.wait_send()


def weight_steps(node, src, dst, sems):
    rows = dst.shape[1]
    half = rows // 2 if node.pair else rows
    offset = pl.multiple_of(node.d * half, half) if node.pair else 0
    mine = pl.ds(offset, half)
    along = {
        s: node.send(
            src.at[pl.ds(pl.multiple_of(node.row(s) * rows + offset, half), half)],
            dst.at[node.r, mine],
            sems,
            s - 1,
            row=node.row(s),
        )
        for s in ORDER
    }
    dst[node.r] = src[span(node.r, rows)]
    yield
    over = []
    for i, s in enumerate(ORDER):
        along[s].wait_recv()
        if node.pair:
            block = dst.at[lax.rem(node.r + 4 - s, 4), mine]
            over.append(node.send(block, block, sems, 3 + i, dp=1 - node.d))
        yield
    for copy in over:
        copy.wait_recv()
    yield
    for copy in list(along.values()) + over:
        copy.wait_send()


def grad_steps(node, src, partner, total, dst, sems, start, done):
    rows = src.shape[1]
    start()
    half = rows // 2 if node.pair else rows
    offset = pl.multiple_of(node.d * half, half) if node.pair else 0
    mine = pl.ds(offset, half)
    if node.pair:
        over = node.send(src.at[:, span(1 - node.d, half)], partner, sems, 0, dp=1 - node.d)
        yield
        over.wait_recv()
    else:
        yield

    def fill(i, _):
        value = src[i, mine]
        if node.pair:
            value = (value.astype(FLT) + partner[i].astype(FLT)).astype(LOW)
        total[i] = value
        return 0

    def place(r):
        return pl.ds(pl.multiple_of(r * rows + offset, half), half)

    back = []

    def send_back(r, i):
        if node.pair:
            block = dst.at[place(r)]
            back.append(node.send(block, block, sems, 4 + i, dp=1 - node.d))

    lax.fori_loop(0, 4, fill, 0)
    along = {
        s: node.send(total.at[node.row(s)], dst.at[place(node.r)], sems, s, row=node.row(s))
        for s in ORDER
    }
    dst[place(node.r)] = total[node.r]
    send_back(node.r, 0)
    yield
    for s in ORDER:
        along[s].wait_recv()
        send_back(lax.rem(node.r + 4 - s, 4), s)
    yield
    for copy in back:
        copy.wait_recv()
    done()
    yield
    for copy in list(along.values()) + back + ([over] if node.pair else []):
        copy.wait_send()


def row_stat_steps(node, box, sums, sems):
    box[node.r] = jnp.broadcast_to(sums, box.shape[1:])
    copies = [
        node.send(box.at[node.r], box.at[node.r], sems, s - 1, row=node.row(s)) for s in (1, 2, 3)
    ]
    for copy in copies:
        copy.wait_recv()
    total = box[0] + box[1] + box[2] + box[3]
    for copy in copies:
        copy.wait_send()
    return total[0:1]


def group_sum_start(node, box, value, sems):
    slot = node.group_slot()
    box[slot] = value
    return [
        node.send(box.at[slot], box.at[slot], sems, i, **where)
        for i, where in enumerate(node.group())
    ]


def box_total(box):
    total = box[0]
    for i in range(1, box.shape[0]):
        total = total + box[i]
    return total


def kernel(dims, pair, names, *refs):
    k = SimpleNamespace(**dict(zip(names, refs, strict=True)))
    node = Node(pair)
    slab, feat, length, units, share = dims.slab, dims.feat, dims.length, dims.units, dims.share
    rows_n = dims.rows
    model = rows_n * feat
    hd = HEAD_DIM
    width = 4 * hd
    scale = HEAD_DIM ** (-0.5)
    tile = slab

    loads = {}
    for i, name in enumerate(LOADED):
        copy = pltpu.make_async_copy(getattr(k, name), getattr(k, name + "_in"), k.loads.at[i])
        copy.start()
        loads[name] = copy
    stores = []

    def store(name):
        copy = pltpu.make_async_copy(
            getattr(k, "f_" + name), getattr(k, name), k.stores.at[len(stores)]
        )
        copy.start()
        stores.append(copy)

    barrier = pltpu.get_barrier_semaphore()
    places = node.group() + [{"row": node.row(s)} for s in (1, 2, 3)]
    for where in places:
        pl.semaphore_signal(
            barrier, inc=1, device_id=where, device_id_type=pl.DeviceIdType.MESH
        )
    for name in ("hidden",) + SMALL:
        loads[name].wait()
    hidden = k.hidden_in[...]
    own_sums = row_sums(hidden * hidden)
    pl.semaphore_wait(barrier, len(places))

    every = []

    def begin(steps):
        every.append(steps)
        next(steps)
        return steps

    def finish(steps):
        for _ in steps:
            pass

    def adv(*many):
        for steps in many:
            next(steps, None)

    def sems(name):
        return (getattr(k, name + "_send"), getattr(k, name + "_recv"))

    def tiles(body):
        lax.fori_loop(0, length // tile, lambda j, _: body(j) or 0, 0)

    total = row_stat_steps(node, k.stat0, own_sums, sems("stat0"))
    rate_in = to_column(lax.rsqrt(total / model + epsilon))
    mine = span(node.c, slab)
    k.g_in[node.r, mine] = (hidden * rate_in * k.norm_in_in[...]).astype(LOW)
    main = begin(gather_steps(node, k.g_in, sems("ag_in"), 2, 3))

    for name in ("w_query", "w_key", "w_value", "w_out"):
        loads[name].wait()
    query_turned = jnp.transpose(k.w_query_in[...])
    key_turned = jnp.transpose(k.w_key_in[...])
    value_turned = jnp.transpose(k.w_value_in[...])
    for r in range(rows_n):
        at = r * width
        head = r // share
        k.wa_src[at : at + hd] = query_turned[r * hd : (r + 1) * hd]
        k.wa_src[at + hd : at + 2 * hd] = key_turned[head * hd : (head + 1) * hd]
        k.wa_src[at + 2 * hd : at + 3 * hd] = value_turned[head * hd : (head + 1) * hd]
        k.wa_src[at + 3 * hd : at + 4 * hd] = k.w_out_in[r * hd : (r + 1) * hd]
    wa_steps = begin(weight_steps(node, k.wa_src, k.wa, sems("wa")))

    loads["cot"].wait()
    k.g_cot[node.r, mine] = k.cot_in[...].astype(LOW)
    documents = k.segments_in[...].astype(FLT)
    document_column = jnp.transpose(jnp.broadcast_to(documents, (128, length)))[:, :1]
    starts = jnp.sum((document_column < documents).astype(FLT), axis=0, keepdims=True)
    k.start[...] = jnp.broadcast_to(starts, k.start.shape).astype(jnp.int32)
    positions = lax.broadcasted_iota(jnp.int32, (1, length), 1).astype(FLT) - starts
    angles = k.frequency_in[...] * positions
    k.cos[...] = jnp.cos(angles)
    k.sin[...] = jnp.sin(angles)
    loads["w_gate"].wait()
    loads["w_up"].wait()
    loads["w_down"].wait()
    for j in range(rows_n * units // 128):
        at = pl.ds(j * 128, 128)
        k.wg_src[at] = jnp.transpose(k.w_gate_in[:, at])
        k.wu_src[at] = jnp.transpose(k.w_up_in[:, at])

    query_gain = jnp.transpose(jnp.broadcast_to(k.query_gain_in[...], (128, hd)))[:, :1]
    key_gain = jnp.transpose(jnp.broadcast_to(k.key_gain_in[...], (128, hd)))[:, :1]
    adv(main, main, main)
    cot_steps = begin(gather_steps(node, k.g_cot, sems("ag_cot"), 1, 1))
    finish(main)
    finish(wa_steps)
    wg_steps = begin(weight_steps(node, k.wg_src, k.wg, sems("wg")))
    adv(cot_steps)
    def project(j):
        cols = span(j, tile)
        acc = nt(k.wa[0, 0 : 3 * hd], k.g_in[0, cols])
        for i in range(1, rows_n):
            acc = acc + nt(k.wa[i, 0 : 3 * hd], k.g_in[i, cols])
        k.raw[:, cols] = acc

    tiles(project)
    adv(cot_steps)
    raw_query, raw_key = k.raw[0:hd], k.raw[hd : 2 * hd]
    cos, sin = k.cos[...], k.sin[...]

    def rotated(raw, gain):
        rate = lax.rsqrt(jnp.mean(raw * raw, axis=0, keepdims=True) + epsilon)
        scaled = raw * rate * gain
        a, b = scaled[: hd // 2], scaled[hd // 2 :]
        return jnp.concatenate([a * cos - b * sin, b * cos + a * sin], axis=0)

    k.qt[...] = rotated(raw_query, query_gain).astype(LOW)
    key_turned = rotated(raw_key, key_gain)
    value_turned = k.raw[2 * hd :]
    k.kt[...] = key_turned.astype(LOW)
    k.vt[...] = value_turned.astype(LOW)
    k.kn[...] = jnp.transpose(key_turned).astype(LOW)
    k.vn[...] = jnp.transpose(value_turned).astype(LOW)
    for j in range(length // tile):
        cols = pl.ds(j * tile, tile)
        ext = (j + 1) * tile
        scores = nn(k.kn[0:ext], k.qt[:, cols]) * scale
        at = lax.broadcasted_iota(jnp.int32, (ext, tile), 0)
        own_place = lax.broadcasted_iota(jnp.int32, (ext, tile), 1) + j * tile
        allowed = (at >= k.start[0:1, cols]) & (at <= own_place)
        raised = jnp.where(allowed, jnp.exp(scores), 0.0)
        probs = raised * (1.0 / jnp.sum(raised, axis=0, keepdims=True))
        k.probs[0:ext, cols] = probs
        k.mixt[:, cols] = nn(k.vt[:, 0:ext], probs.astype(LOW))
        adv(cot_steps)
    k.mix[...] = jnp.transpose(k.mixt[...]).astype(LOW)
    def out_part(r):
        def body(j):
            rows = span(j, tile)
            k.part[r, rows] = nn(k.mix[rows], k.wa[r, 3 * hd :]).astype(LOW)

        tiles(body)

    def take(total):
        k.blk[...] = total

    def bufs(name, second=""):
        return (
            getattr(k, "part" + second),
            getattr(k, name + "_got"),
            getattr(k, "passed" + second),
            getattr(k, name + "_far"),
            getattr(k, "leave" + second),
            getattr(k, name + "_arr"),
            getattr(k, "carry" + second),
        )

    main = begin(reduce_steps(node, bufs("ro"), sems("ro"), 2, out_part, take))
    adv(main, main, main, main, main, main, main)
    wu_steps = begin(weight_steps(node, k.wu_src, k.wu, sems("wu")))
    adv(cot_steps)
    adv(main, main)
    adv(cot_steps)
    adv(main, main)
    adv(cot_steps)
    wd_steps = begin(weight_steps(node, k.w_down_in, k.wd, sems("wd")))
    finish(main)
    resid = k.hidden_in[...] + k.blk[...]
    k.resid[...] = resid
    total = row_stat_steps(node, k.stat1, row_sums(resid * resid), sems("stat1"))
    rate_mid = to_column(lax.rsqrt(total / model + epsilon))
    k.rate_mid[...] = jnp.broadcast_to(rate_mid, k.rate_mid.shape)
    k.rate_in[...] = jnp.broadcast_to(rate_in, k.rate_in.shape)
    k.g_mid[node.r, mine] = (resid * rate_mid * k.norm_mid_in[...]).astype(LOW)
    def ff_in(r, i):
        def body(j):
            cols = span(j, tile)
            gate = nt(k.wg[r], k.g_mid[r, cols])
            up = nt(k.wu[r], k.g_mid[r, cols])
            if i:
                gate = gate + k.gate[:, cols]
                up = up + k.up[:, cols]
            k.gate[:, cols] = gate
            k.up[:, cols] = up

        tiles(body)

    def mid_done(r, i):
        if i == 0:
            finish(wg_steps)
            finish(wu_steps)
        if i == 2:
            finish(wd_steps)
            finish(cot_steps)

            def body(j):
                cols = span(j, tile)
                acc = nt(k.wd[0], k.g_cot[0, cols])
                for i in range(1, rows_n):
                    acc = acc + nt(k.wd[i], k.g_cot[i, cols])
                k.gsw[:, cols] = acc

            tiles(body)
        ff_in(r, i)

    main = begin(gather_steps(node, k.g_mid, sems("ag_mid"), 2, 3, mid_done))
    adv(wg_steps, wg_steps, wg_steps, cot_steps)
    adv(main)
    adv(wu_steps, wu_steps, wu_steps, cot_steps)
    adv(main, main, main)
    adv(wd_steps, wd_steps, wd_steps, cot_steps)
    finish(main)
    def activate(j):
        cols = span(j, tile)
        gate, up, gsw = k.gate[:, cols], k.up[:, cols], k.gsw[:, cols]
        sig = 1.0 / (1.0 + jnp.exp(-gate))
        act = gate * sig
        sw = act * up
        gga = gsw * up * sig * (1.0 + gate * (1.0 - sig))
        gua = gsw * act
        k.sw[:, cols] = sw.astype(LOW)
        k.gga[:, cols] = gga.astype(LOW)
        k.gua[:, cols] = gua.astype(LOW)
        k.sw_t[cols] = jnp.transpose(sw).astype(LOW)
        k.gga_t[cols] = jnp.transpose(gga).astype(LOW)
        k.gua_t[cols] = jnp.transpose(gua).astype(LOW)

    tiles(activate)
    def mid_part(r):
        def body(j):
            rows = span(j, tile)
            k.part[r, rows] = (nn(k.gga_t[rows], k.wg[r]) + nn(k.gua_t[rows], k.wu[r])).astype(LOW)

        tiles(body)

    def down_part(r):
        def body(j):
            rows = span(j, tile)
            k.part2[r, rows] = nn(k.sw_t[rows], k.wd[r]).astype(LOW)

        tiles(body)

    def outer(left, whole, target):
        def start():
            def body(i, _):
                target[i] = nn(left[...], whole[i]).astype(LOW)
                return 0

            lax.fori_loop(0, rows_n, body, 0)

        return start

    def turned_out(source, target, name):
        def done():
            for j in range(rows_n * units // 128):
                at = pl.ds(j * 128, 128)
                target[:, at] = jnp.transpose(source[at].astype(FLT))
            store(name)

        return done

    def down_out():
        k.f_grad_down[...] = k.od[...].astype(FLT)
        store("grad_down")

    gd_steps = grad_steps(
        node, k.gs_d, k.yb_d, k.gr_d, k.od, sems("gd"), outer(k.sw, k.g_cot, k.gs_d), down_out
    )
    gg_steps = grad_steps(
        node, k.gs_g, k.yb_g, k.gr_g, k.og, sems("gg"), outer(k.gga, k.g_mid, k.gs_g),
        turned_out(k.og, k.f_grad_gate, "grad_gate"),
    )
    gu_steps = grad_steps(
        node, k.gs_u, k.yb_u, k.gr_u, k.ou, sems("gu"), outer(k.gua, k.g_mid, k.gs_u),
        turned_out(k.ou, k.f_grad_up, "grad_up"),
    )

    def put_output(total):
        k.f_output[...] = k.resid[...] + total
        store("output")

    main = begin(reduce_steps(node, bufs("rm"), sems("rm"), 2, mid_part, take))
    adv(main, main, main, main, main, main, main)
    begin(gd_steps)
    adv(main)
    begin(gg_steps)
    adv(main)
    begin(gu_steps)
    adv(main, main)
    adv(gd_steps)
    adv(main, main)
    finish(main)
    down_steps = reduce_steps(node, bufs("rd", "2"), sems("rd"), 1, down_part, put_output)
    grad_normed_mid = k.blk[...]
    resid = k.resid[...]
    rate_mid = k.rate_mid[:, 0:1]
    scaled = k.norm_mid_in[...] * grad_normed_mid
    total = row_stat_steps(node, k.stat2, row_sums(scaled * resid), sems("stat2"))
    grad_resid = k.cot_in[...] + rate_mid * scaled - resid * (
        rate_mid * rate_mid * rate_mid * to_column(total / model)
    )
    k.grad_resid[...] = grad_resid
    k.g_res[node.r, mine] = grad_resid.astype(LOW)
    main = begin(gather_steps(node, k.g_res, sems("ag_res"), 2, 3))
    begin(down_steps)
    gain_mid = jnp.sum(grad_normed_mid * resid * rate_mid, axis=0, keepdims=True)
    adv(main)
    adv(gg_steps)
    adv(main)
    adv(down_steps, down_steps)
    adv(main, main)
    adv(gd_steps, gu_steps)
    adv(down_steps, down_steps, down_steps)
    adv(main, main, main)
    adv(gg_steps)
    finish(main)
    def grad_mixed(j):
        cols = span(j, tile)
        acc = nt(k.wa[0, 3 * hd :], k.g_res[0, cols])
        for i in range(1, rows_n):
            acc = acc + nt(k.wa[i, 3 * hd :], k.g_res[i, cols])
        k.gmt[:, cols] = acc.astype(LOW)

    tiles(grad_mixed)
    k.dk[...] = jnp.zeros(k.dk.shape, FLT)
    k.dv[...] = jnp.zeros(k.dv.shape, FLT)
    for j in range(length // tile):
        cols = pl.ds(j * tile, tile)
        ext = (j + 1) * tile
        probs = k.probs[0:ext, cols]
        k.dv[:, 0:ext] += nt(k.gmt[:, cols], probs.astype(LOW))
        grad_probs = nn(k.vn[0:ext], k.gmt[:, cols])
        inner = jnp.sum(probs * grad_probs, axis=0, keepdims=True)
        grad_scores = (probs * (grad_probs - inner) * scale).astype(LOW)
        k.dq[:, cols] = nn(k.kt[:, 0:ext], grad_scores)
        k.dk[:, 0:ext] += nt(k.qt[:, cols], grad_scores)
        adv(down_steps)

    def turned_back(grad, raw, gain):
        rate = lax.rsqrt(jnp.mean(raw * raw, axis=0, keepdims=True) + epsilon)
        a, b = grad[: hd // 2], grad[hd // 2 :]
        t = jnp.concatenate([a * cos + b * sin, b * cos - a * sin], axis=0)
        scaled = gain * t
        inner = jnp.mean(scaled * raw, axis=0, keepdims=True)
        return (
            rate * scaled - raw * (rate * rate * rate * inner),
            jnp.sum(t * raw * rate, axis=1, keepdims=True),
        )

    cos, sin = k.cos[...], k.sin[...]
    grad_query, gain_query = turned_back(k.dq[...], k.raw[0:hd], query_gain)
    grad_key, gain_key = turned_back(k.dk[...], k.raw[hd : 2 * hd], key_gain)
    grad_proj = jnp.concatenate([grad_query, grad_key, k.dv[...]], axis=0)
    k.gp_turned[...] = grad_proj.astype(LOW)
    k.gp[...] = jnp.transpose(grad_proj).astype(LOW)
    def in_part(r):
        def body(j):
            rows = span(j, tile)
            k.part[r, rows] = nn(k.gp[rows], k.wa[r, 0 : 3 * hd]).astype(LOW)

        tiles(body)

    def outer_attention():
        def body(i, _):
            k.gs_a[i, 0 : 3 * hd] = nn(k.gp_turned[...], k.g_in[i]).astype(LOW)
            k.gs_a[i, 3 * hd :] = nn(k.mixt[...].astype(LOW), k.g_res[i]).astype(LOW)
            return 0

        lax.fori_loop(0, rows_n, body, 0)

    def attention_out():
        def part(r, i):
            return k.oa[r * width + i * hd : r * width + (i + 1) * hd].astype(FLT)

        k.f_grad_query[...] = jnp.transpose(
            jnp.concatenate([part(r, 0) for r in range(rows_n)], axis=0)
        )
        for i, target in ((1, k.f_grad_key), (2, k.f_grad_value)):
            heads = []
            for h in range(rows_n // share):
                acc = part(h * share, i)
                for r in range(h * share + 1, (h + 1) * share):
                    acc = acc + part(r, i)
                heads.append(acc)
            target[...] = jnp.transpose(jnp.concatenate(heads, axis=0))
        for r in range(rows_n):
            k.f_grad_out[r * hd : (r + 1) * hd] = part(r, 3)
        for name in ("grad_query", "grad_key", "grad_value", "grad_out"):
            store(name)

    ga_steps = grad_steps(
        node, k.gs_a, k.yb_a, k.gr_a, k.oa, sems("ga"), outer_attention, attention_out
    )
    main = begin(reduce_steps(node, bufs("ri"), sems("ri"), 2, in_part, take))
    k.gains[...] = jnp.zeros(k.gains.shape, FLT)
    k.gains[0:1, :] = gain_mid
    k.gains[1:2, 0:hd] = to_row(gain_query)
    k.gains[2:3, 0:hd] = to_row(gain_key)
    gain_copies = group_sum_start(node, k.gbox, k.gains[...], sems("gbox"))
    adv(main, main, main, main, main, main, main)
    begin(ga_steps)
    adv(gu_steps)
    adv(main, main)
    adv(ga_steps)
    adv(main, main)
    adv(gd_steps, gg_steps, gu_steps)
    adv(main, main)
    finish(main)
    adv(ga_steps)
    grad_normed_in = k.blk[...]
    rate_in = k.rate_in[:, 0:1]
    hidden = k.hidden_in[...]
    gain_in = jnp.sum(grad_normed_in * hidden * rate_in, axis=0, keepdims=True)
    in_copies = group_sum_start(
        node, k.inbox, jnp.broadcast_to(gain_in, k.gains.shape), sems("inbox")
    )
    for copy in gain_copies:
        copy.wait_recv()
    gains = box_total(k.gbox)
    k.f_gain_mid[...] = gains[0:1]
    store("gain_mid")
    k.qkbox[node.r] = gains
    qk_copies = [
        node.send(k.qkbox.at[node.r], k.qkbox.at[node.r], sems("qkbox"), s - 1, row=node.row(s))
        for s in (1, 2, 3)
    ]
    scaled = k.norm_in_in[...] * grad_normed_in
    total = row_stat_steps(node, k.stat3, row_sums(scaled * hidden), sems("stat3"))
    k.f_grad_hidden[...] = (
        k.grad_resid[...] + rate_in * scaled - hidden * (rate_in * rate_in * rate_in * to_column(total / model))
    )
    store("grad_hidden")
    finish(down_steps)
    for steps in (gd_steps, gg_steps, gu_steps, ga_steps):
        finish(steps)
    for copy in qk_copies:
        copy.wait_recv()
    gains = box_total(k.qkbox)
    k.f_gain_query[...] = gains[1:2, 0:hd]
    k.f_gain_key[...] = gains[2:3, 0:hd]
    store("gain_query")
    store("gain_key")
    for copy in in_copies:
        copy.wait_recv()
    k.f_gain_in[...] = box_total(k.inbox)[0:1]
    store("gain_in")
    for copy in gain_copies + qk_copies + in_copies:
        copy.wait_send()
    for copy in stores:
        copy.wait()


def copy_kernel(count, *refs):
    held, arrive, leave = refs[2 * count : 3 * count], refs[-2], refs[-1]
    inward = [pltpu.make_async_copy(refs[i], held[i], arrive.at[i]) for i in range(count)]
    outward = [
        pltpu.make_async_copy(held[i], refs[count + i], leave.at[i]) for i in range(count)
    ]
    for copy in inward:
        copy.start()
    for came, left in zip(inward, outward):
        came.wait()
        left.start()
    for copy in outward:
        copy.wait()


SMALL = ("norm_in", "segments", "frequency", "query_gain", "key_gain", "norm_mid")
LARGE = ("w_query", "w_key", "w_value", "w_out", "cot", "w_gate", "w_up", "w_down")
LOADED = ("hidden",) + SMALL + LARGE


def local(
    hidden_in,
    segments,
    norm_in,
    w_query,
    w_key,
    w_value,
    query_gain,
    key_gain,
    w_out,
    norm_mid,
    w_gate,
    w_up,
    w_down,
    cotangent,
):
    rows, cols, dps = lax.axis_size("row"), lax.axis_size("col"), lax.axis_size("dp")
    pair = dps == 2
    slab, feat = hidden_in.shape
    length = segments.shape[1]
    hd = HEAD_DIM
    q_cols, k_cols, u_cols = w_query.shape[1], w_key.shape[1], w_gate.shape[1]
    share = rows * hd // k_cols
    units = u_cols // rows
    assert rows == 4 and cols == 4 and q_cols == rows * hd and slab * cols == length
    dims = SimpleNamespace(
        slab=slab, feat=feat, length=length, units=units, share=share, rows=rows
    )
    powers = np.arange(hd // 2, dtype=np.float64) * (-2.0 / hd)
    frequency = jnp.asarray((rope_base**powers).astype(np.float32)[:, None])
    shape = jax.ShapeDtypeStruct
    small = dict(
        segments=segments,
        norm_in=norm_in[None, :],
        norm_mid=norm_mid[None, :],
        query_gain=query_gain[None, :],
        key_gain=key_gain[None, :],
        frequency=frequency,
    )
    large = dict(
        hidden=hidden_in,
        cot=cotangent,
        w_query=w_query,
        w_key=w_key,
        w_value=w_value,
        w_out=w_out,
        w_gate=w_gate,
        w_up=w_up,
        w_down=w_down,
    )
    block = (slab, feat)
    large_outs = dict(
        output=block,
        grad_hidden=block,
        grad_query=w_query.shape,
        grad_key=w_key.shape,
        grad_value=w_value.shape,
        grad_out=w_out.shape,
        grad_gate=w_gate.shape,
        grad_up=w_up.shape,
        grad_down=w_down.shape,
    )
    small_outs = dict(
        gain_mid=(1, feat), gain_in=(1, feat), gain_query=(1, hd), gain_key=(1, hd)
    )
    width = 4 * hd
    low = lambda *dims: pltpu.VMEM(dims, LOW)
    flt = lambda *dims: pltpu.VMEM(dims, FLT)
    group = cols * (2 if pair else 1)
    scratch = {
        name + "_in": pltpu.VMEM(array.shape, array.dtype)
        for name, array in (small | large).items()
    }
    scratch.update({"f_" + name: flt(*dims) for name, dims in (small_outs | large_outs).items()})
    scratch.update(
        loads=pltpu.SemaphoreType.DMA((len(LOADED),)),
        stores=pltpu.SemaphoreType.DMA((len(small_outs) + len(large_outs),)),
        wa_src=low(rows * width, feat),
        wg_src=low(rows * units, feat),
        wu_src=low(rows * units, feat),
        resid=flt(slab, feat),
        grad_resid=flt(slab, feat),
        blk=flt(slab, feat),
        carry=flt(slab, feat),
        carry2=flt(slab, feat),
        rate_in=flt(slab, 128),
        rate_mid=flt(slab, 128),
        start=pltpu.VMEM((8, length), jnp.int32),
        cos=flt(hd // 2, length),
        sin=flt(hd // 2, length),
        wa=low(rows, width, feat),
        wg=low(rows, units, feat),
        wu=low(rows, units, feat),
        wd=low(rows, units, feat),
        part=low(rows, length, feat),
        part2=low(rows, length, feat),
        passed=low(rows, slab, feat),
        passed2=low(rows, slab, feat),
        leave=low(rows - 1, slab, feat),
        leave2=low(rows - 1, slab, feat),
        raw=flt(3 * hd, length),
        qt=low(hd, length),
        kt=low(hd, length),
        vt=low(hd, length),
        kn=low(length, hd),
        vn=low(length, hd),
        probs=flt(length, length),
        mixt=flt(hd, length),
        mix=low(length, hd),
        gmt=low(hd, length),
        dq=flt(hd, length),
        dk=flt(hd, length),
        dv=flt(hd, length),
        gp_turned=low(3 * hd, length),
        gp=low(length, 3 * hd),
        gate=flt(units, length),
        up=flt(units, length),
        gsw=flt(units, length),
        sw=low(units, length),
        gga=low(units, length),
        gua=low(units, length),
        sw_t=low(length, units),
        gga_t=low(length, units),
        gua_t=low(length, units),
        gains=flt(8, feat),
        gbox=flt(group, 8, feat),
        inbox=flt(group, 8, feat),
        qkbox=flt(rows, 8, feat),
    )
    counts = dict(gbox=group - 1, inbox=group - 1, qkbox=3)
    for name in ("stat0", "stat1", "stat2", "stat3"):
        scratch[name] = flt(rows, 8, slab)
        counts[name] = 3
    for name in ("in", "cot", "mid", "res"):
        scratch["g_" + name] = low(rows, length, feat)
        counts["ag_" + name] = 17 * (1 if name == "cot" else 2)
    for name in ("ro", "rm", "rd", "ri"):
        scratch[name + "_got"] = low(rows, 2, slab, feat)
        scratch[name + "_far"] = low(rows, slab, feat)
        scratch[name + "_arr"] = low(rows + 1, slab, feat)
        pieces = 1 if name == "rd" else 2
        counts[name] = 13 * pieces + 4
    for name, size in (("a", width), ("g", units), ("u", units), ("d", units)):
        half = size // 2 if pair else size
        scratch["gs_" + name] = low(rows, size, feat)
        scratch["yb_" + name] = low(rows, half, feat)
        scratch["gr_" + name] = low(rows, half, feat)
        scratch["o" + name] = low(rows * size, feat)
        counts["w" + name] = 6
        counts["g" + name] = 8
    for name, count in counts.items():
        scratch[name + "_send"] = pltpu.SemaphoreType.DMA((count,))
        scratch[name + "_recv"] = pltpu.SemaphoreType.DMA((count,))
    anywhere = pl.BlockSpec(memory_space=pl.ANY)
    names = tuple(small) + tuple(large) + tuple(small_outs) + tuple(large_outs) + tuple(scratch)
    out_shape = tuple(shape(d, FLT) for d in (small_outs | large_outs).values())
    got = pl.pallas_call(
        functools.partial(kernel, dims, pair, names),
        out_shape=out_shape,
        in_specs=[anywhere] * (len(small) + len(large)),
        out_specs=(anywhere,) * len(out_shape),
        scratch_shapes=list(scratch.values()),
        compiler_params=pltpu.CompilerParams(
            collective_id=0, has_side_effects=True, vmem_limit_bytes=60 * 2**20
        ),
    )(*small.values(), *large.values())
    if pair:
        got = pl.pallas_call(
            functools.partial(copy_kernel, len(got)),
            out_shape=out_shape,
            in_specs=[anywhere] * len(got),
            out_specs=(anywhere,) * len(got),
            scratch_shapes=[pltpu.VMEM(array.shape, array.dtype) for array in got]
            + [pltpu.SemaphoreType.DMA((len(got),))] * 2,
        )(*got)
    o = SimpleNamespace(**dict(zip(tuple(small_outs) + tuple(large_outs), got, strict=True)))
    if not pair:
        for name in tuple(small_outs) + tuple(large_outs)[2:]:
            setattr(o, name, lax.psum(getattr(o, name), "dp"))
    return (
        o.output,
        o.grad_hidden,
        o.gain_in[0],
        o.grad_query,
        o.grad_key,
        o.grad_value,
        o.gain_query[0],
        o.gain_key[0],
        o.grad_out,
        o.gain_mid[0],
        o.grad_gate,
        o.grad_up,
        o.grad_down,
    )


def solution(mesh):
    stream = P(("dp", "col"), "row")
    first, last = P("row", "col"), P("col", "row")
    return jax.shard_map(
        local,
        mesh=mesh,
        in_specs=(stream, P("dp", None), P("row"), first, first, first, P(), P(), last, P("row"), first, first, last, stream),
        out_specs=(stream, stream, P("row"), first, first, first, P(), P(), last, P("row"), first, first, last),
        check_vma=False,
    )
```

```python
import functools
from types import SimpleNamespace

import jax
import jax.numpy as jnp
import numpy as np
from jax import lax
from jax.experimental import pallas as pl
from jax.experimental.pallas import tpu as pltpu
from jax.sharding import PartitionSpec as P

HEAD_DIM = 64
epsilon = 1e-05
rope_base = 1000000.0
LOW = jnp.bfloat16
FLT = jnp.float32
ORDER = (1, 3, 2)


def nn(left_side, right_side):
    return jnp.dot(left_side, right_side, preferred_element_type=FLT)


def nt(left_side, right_side):
    return lax.dot_general(
        left_side, right_side, (((1,), (1,)), ((), ())), preferred_element_type=FLT
    )


def row_sums(block):
    return jnp.sum(jnp.transpose(block), axis=0, keepdims=True)


def to_column(row):
    return jnp.transpose(jnp.broadcast_to(row, (128, row.shape[1])))[:, :1]


def to_row(column):
    return jnp.transpose(jnp.broadcast_to(column, (column.shape[0], 128)))[:1, :]


class Node:
    def __init__(self, pair):
        self.pair = pair
        self.r = lax.axis_index("row")
        self.c = lax.axis_index("col")
        self.d = lax.axis_index("dp")
        self.near = self.c + 1 - 2 * lax.rem(self.c, 2)
        self.far = lax.rem(self.c + 2, 4)
        self.across = lax.rem(self.near + 2, 4)
        self.inner = lax.rem((self.r + 1) // 2, 2)
        self.inward = 1 + lax.rem(self.r, 2)
        self.outward = 3 * (self.r // 2)
        self.third = 3 - 3 * (self.r // 2)
        self.second = 2 - self.r // 2
        self.first = self.r + 1 - 2 * lax.rem(self.r, 2)

    def row(self, step):
        return lax.rem(self.r + step, 4)

    def send(self, src, dst, sems, slot, start=True, **where):
        copy = pltpu.make_async_remote_copy(
            src_ref=src,
            dst_ref=dst,
            send_sem=sems[0].at[slot[0] if isinstance(slot, tuple) else slot],
            recv_sem=sems[1].at[slot[1] if isinstance(slot, tuple) else slot],
            device_id=where,
            device_id_type=pl.DeviceIdType.MESH,
        )
        if start:
            copy.start()
        return copy

    def group(self):
        places = []
        for dp_step in range(2 if self.pair else 1):
            for col_step in range(4):
                if dp_step + col_step:
                    where = {"col": lax.rem(self.c + col_step, 4)}
                    if self.pair:
                        where["dp"] = lax.rem(self.d + dp_step, 2)
                    places.append(where)
        return places

    def group_slot(self):
        return self.d * 4 + self.c if self.pair else self.c


def span(block, size):
    return pl.ds(pl.multiple_of(block * size, size), size)


def gather_steps(node, whole, sems, pieces, lag, done=None):
    size = whole.shape[1] // 4
    cut = size // pieces

    def here(r, c, h):
        return whole.at[r, pl.ds(pl.multiple_of(c * size + h * cut, cut), cut)]

    def along(slot, origin, h, to, start=True):
        block = here(origin, node.c, h)
        return node.send(
            block, block, sems, (slot * pieces + h, origin * pieces + h), start, row=to
        )

    def when_inner(slot, origin, h, to):
        @pl.when(node.inner == 1)
        def _():
            along(slot, origin, h, to)

    rows = [node.r, node.first, node.second, node.third]
    near, far, relay = {}, {}, {}
    waiting = []

    def spread(i, h):
        block = here(rows[i], node.c, h)
        far[i, h] = node.send(block, block, sems, 9 * pieces + i * pieces + h, col=node.far)
        near[i, h] = node.send(block, block, sems, 5 * pieces + i * pieces + h, col=node.near)
        waiting.append((i, h))

    def pass_on():
        i, h = waiting.pop(0)
        far[i, h].wait_recv()
        block = here(rows[i], node.far, h)
        relay[i, h] = node.send(block, block, sems, 13 * pieces + i * pieces + h, col=node.near)

    def complete(i):
        for h in range(pieces):
            near[i, h].wait_recv()
            relay[i, h].wait_recv()
        if done is not None:
            done(rows[i], i)

    onward = {1: node.inward, 2: node.outward, 3: node.outward}
    own = []
    for h in range(pieces):
        own.append(along(0, node.r, h, node.inward))
        when_inner(1, node.r, h, node.outward)
        spread(0, h)
    yield
    for i in (1, 2, 3):
        for h in range(pieces):
            along(0, rows[i], h, node.inward, start=False).wait_recv()
            when_inner(1 + i, rows[i], h, onward[i])
            spread(i, h)
            while len(waiting) > lag:
                pass_on()
            yield
        if i >= 2:
            while waiting[0][0] <= i - 2:
                pass_on()
            complete(i - 2)
            yield
    for i in (2, 3):
        while waiting and waiting[0][0] <= i:
            pass_on()
        complete(i)
        yield
    for copy in own:
        copy.wait_send()

    @pl.when(node.inner == 1)
    def _():
        for h in range(pieces):
            along(1, node.r, h, node.outward, start=False).wait_send()
            for i in (1, 2, 3):
                along(1 + i, rows[i], h, onward[i], start=False).wait_send()

    for copy in list(near.values()) + list(far.values()) + list(relay.values()):
        copy.wait_send()


def reduce_steps(node, bufs, sems, pieces, compute, finish):
    part, got, passed, from_far, out, arrived, carry = bufs
    size = part.shape[1] // 4
    cut = size // pieces
    rows = [node.third, node.second, node.first, node.r]
    first, second, crossing, along = {}, {}, {}, {}
    to = {0: node.inward, 1: node.inward, 2: node.inward + node.inner * (node.outward - node.inward)}
    slot_there = {0: 2 * node.inner, 1: 1 + 2 * node.inner, 2: 4 - node.inner}

    def piece(c, h):
        return pl.ds(pl.multiple_of(c * size + h * cut, cut), cut)

    def begin(i):
        compute(rows[i])
        for h in range(pieces):
            first[i, h] = node.send(
                part.at[rows[i], piece(node.across, h)],
                got.at[i, 0, pl.ds(h * cut, cut)],
                sems,
                i * pieces + h,
                col=node.near,
            )
        second[i] = node.send(
            part.at[rows[i], span(node.near, size)], got.at[i, 1], sems, 4 * pieces + i, col=node.near
        )

    def cross(i):
        for h in range(pieces):
            at = pl.ds(h * cut, cut)
            first[i, h].wait_recv()
            passed[i, at] = (
                part[rows[i], piece(node.far, h)].astype(FLT) + got[i, 0, at].astype(FLT)
            ).astype(LOW)
            crossing[i, h] = node.send(
                passed.at[i, at],
                from_far.at[i, at],
                sems,
                4 * pieces + 4 + i * pieces + h,
                col=node.far,
            )

    base = 8 * pieces + 4

    def add_arrived(slot, h):
        at = pl.ds(h * cut, cut)
        node.send(
            out.at[0, at],
            arrived.at[slot, at],
            sems,
            (base, base + slot * pieces + h),
            False,
            row=node.inward,
        ).wait_recv()
        carry[at] += arrived[slot, at].astype(FLT)

    def close(i, h):
        at = pl.ds(h * cut, cut)
        if h == 0:
            second[i].wait_recv()
        crossing[i, h].wait_recv()
        carry[at] = (
            part[rows[i], piece(node.c, h)].astype(FLT)
            + got[i, 1, at].astype(FLT)
            + from_far[i, at].astype(FLT)
        )
        if i == 3:
            add_arrived(3, h)

        @pl.when(node.inner == 1)
        def _():
            add_arrived(4 if i == 3 else i, h)

        if i < 3:
            out[i, at] = carry[at].astype(LOW)
            along[i, h] = node.send(
                out.at[i, at],
                arrived.at[slot_there[i], at],
                sems,
                (base + i * pieces + h, base + slot_there[i] * pieces + h),
                row=to[i],
            )

    for i in range(4):
        begin(i)
        yield
        if i >= 1:
            cross(i - 1)
            yield
    cross(3)
    yield
    for i in range(4):
        for h in range(pieces):
            close(i, h)
            yield
    finish(carry[...])
    yield
    for group in (first, second, crossing, along):
        for copy in group.values():
            copy.wait_send()


def weight_steps(node, src, dst, sems):
    rows = dst.shape[1]
    half = rows // 2 if node.pair else rows
    offset = pl.multiple_of(node.d * half, half) if node.pair else 0
    mine = pl.ds(offset, half)
    along = {
        s: node.send(
            src.at[pl.ds(pl.multiple_of(node.row(s) * rows + offset, half), half)],
            dst.at[node.r, mine],
            sems,
            s - 1,
            row=node.row(s),
        )
        for s in ORDER
    }
    dst[node.r] = src[span(node.r, rows)]
    yield
    over = []
    for i, s in enumerate(ORDER):
        along[s].wait_recv()
        if node.pair:
            block = dst.at[lax.rem(node.r + 4 - s, 4), mine]
            over.append(node.send(block, block, sems, 3 + i, dp=1 - node.d))
        yield
    for copy in over:
        copy.wait_recv()
    yield
    for copy in list(along.values()) + over:
        copy.wait_send()


def grad_steps(node, src, partner, total, dst, sems, start, done):
    rows = src.shape[1]
    start()
    half = rows // 2 if node.pair else rows
    offset = pl.multiple_of(node.d * half, half) if node.pair else 0
    mine = pl.ds(offset, half)
    if node.pair:
        over = node.send(src.at[:, span(1 - node.d, half)], partner, sems, 0, dp=1 - node.d)
        yield
        over.wait_recv()
    else:
        yield

    def fill(i, _):
        value = src[i, mine]
        if node.pair:
            value = (value.astype(FLT) + partner[i].astype(FLT)).astype(LOW)
        total[i] = value
        return 0

    def place(r):
        return pl.ds(pl.multiple_of(r * rows + offset, half), half)

    back = []

    def send_back(r, i):
        if node.pair:
            block = dst.at[place(r)]
            back.append(node.send(block, block, sems, 4 + i, dp=1 - node.d))

    lax.fori_loop(0, 4, fill, 0)
    along = {
        s: node.send(total.at[node.row(s)], dst.at[place(node.r)], sems, s, row=node.row(s))
        for s in ORDER
    }
    dst[place(node.r)] = total[node.r]
    send_back(node.r, 0)
    yield
    for s in ORDER:
        along[s].wait_recv()
        send_back(lax.rem(node.r + 4 - s, 4), s)
    yield
    for copy in back:
        copy.wait_recv()
    done()
    yield
    for copy in list(along.values()) + back + ([over] if node.pair else []):
        copy.wait_send()


def row_stat_start(node, box, sums, sems):
    box[node.r] = jnp.broadcast_to(sums, box.shape[1:])
    return [
        node.send(box.at[node.r], box.at[node.r], sems, s - 1, row=node.row(s)) for s in (1, 2, 3)
    ]


def row_stat_end(box, copies):
    for copy in copies:
        copy.wait_recv()
    total = box[0] + box[1] + box[2] + box[3]
    for copy in copies:
        copy.wait_send()
    return total[0:1]


def row_stat_steps(node, box, sums, sems):
    return row_stat_end(box, row_stat_start(node, box, sums, sems))


def rates_start(node, wide, rates, sems):
    wide[node.c] = jnp.broadcast_to(rates, wide.shape[1:])
    return [
        node.send(wide.at[node.c], wide.at[node.c], sems, 2 + s, col=lax.rem(node.c + s, 4))
        for s in (1, 2, 3)
    ]


def rates_end(wide, target, copies):
    for copy in copies:
        copy.wait_recv()
    size = wide.shape[2]
    for i in range(wide.shape[0]):
        target[:, i * size : (i + 1) * size] = wide[i]
    for copy in copies:
        copy.wait_send()


def group_sum_start(node, box, value, sems):
    slot = node.group_slot()
    box[slot] = value
    return [
        node.send(box.at[slot], box.at[slot], sems, i, **where)
        for i, where in enumerate(node.group())
    ]


def box_total(box):
    total = box[0]
    for i in range(1, box.shape[0]):
        total = total + box[i]
    return total


def kernel(dims, pair, names, *refs):
    k = SimpleNamespace(**dict(zip(names, refs, strict=True)))
    node = Node(pair)
    slab, feat, length, units, share = dims.slab, dims.feat, dims.length, dims.units, dims.share
    rows_n = dims.rows
    model = rows_n * feat
    hd = HEAD_DIM
    width = 4 * hd
    scale = HEAD_DIM ** (-0.5)
    tile = slab

    loads = {}
    for i, name in enumerate(LOADED):
        copy = pltpu.make_async_copy(getattr(k, name), getattr(k, name + "_in"), k.loads.at[i])
        copy.start()
        loads[name] = copy
    stores = []

    def store(name):
        copy = pltpu.make_async_copy(
            getattr(k, "f_" + name), getattr(k, name), k.stores.at[len(stores)]
        )
        copy.start()
        stores.append(copy)

    barrier = pltpu.get_barrier_semaphore()
    places = node.group() + [{"row": node.row(s)} for s in (1, 2, 3)]
    for where in places:
        pl.semaphore_signal(
            barrier, inc=1, device_id=where, device_id_type=pl.DeviceIdType.MESH
        )
    for name in ("hidden",) + SMALL:
        loads[name].wait()
    hidden = k.hidden_in[...]
    own_sums = row_sums(hidden * hidden)
    pl.semaphore_wait(barrier, len(places))

    every = []

    def begin(steps):
        every.append(steps)
        next(steps)
        return steps

    def finish(steps):
        for _ in steps:
            pass

    def adv(*many):
        for steps in many:
            next(steps, None)

    def sems(name):
        return (getattr(k, name + "_send"), getattr(k, name + "_recv"))

    def tiles(body):
        lax.fori_loop(0, length // tile, lambda j, _: body(j) or 0, 0)

    mine = span(node.c, slab)
    stat_copies = row_stat_start(node, k.stat0, own_sums, sems("stat0"))
    k.g_in[node.r, mine] = (hidden * k.norm_in_in[...]).astype(LOW)
    main = begin(gather_steps(node, k.g_in, sems("ag_in"), 2, 3))

    for name in ("w_query", "w_key", "w_value", "w_out"):
        loads[name].wait()
    query_turned = jnp.transpose(k.w_query_in[...])
    key_turned = jnp.transpose(k.w_key_in[...])
    value_turned = jnp.transpose(k.w_value_in[...])
    for r in range(rows_n):
        at = r * width
        head = r // share
        k.wa_src[at : at + hd] = query_turned[r * hd : (r + 1) * hd]
        k.wa_src[at + hd : at + 2 * hd] = key_turned[head * hd : (head + 1) * hd]
        k.wa_src[at + 2 * hd : at + 3 * hd] = value_turned[head * hd : (head + 1) * hd]
        k.wa_src[at + 3 * hd : at + 4 * hd] = k.w_out_in[r * hd : (r + 1) * hd]
    wa_steps = begin(weight_steps(node, k.wa_src, k.wa, sems("wa")))

    rates = lax.rsqrt(row_stat_end(k.stat0, stat_copies) / model + epsilon)
    k.rate_in[...] = jnp.broadcast_to(to_column(rates), k.rate_in.shape)
    rate_copies = rates_start(node, k.wide0, rates, sems("stat0"))
    loads["cot"].wait()
    k.g_cot[node.r, mine] = k.cot_in[...].astype(LOW)
    documents = k.segments_in[...].astype(FLT)
    document_column = jnp.transpose(jnp.broadcast_to(documents, (128, length)))[:, :1]
    starts = jnp.sum((document_column < documents).astype(FLT), axis=0, keepdims=True)
    k.start[...] = jnp.broadcast_to(starts, k.start.shape).astype(jnp.int32)
    positions = lax.broadcasted_iota(jnp.int32, (1, length), 1).astype(FLT) - starts
    angles = k.frequency_in[...] * positions
    k.cos[...] = jnp.cos(angles)
    k.sin[...] = jnp.sin(angles)
    loads["w_gate"].wait()
    loads["w_up"].wait()
    loads["w_down"].wait()
    for j in range(rows_n * units // 128):
        at = pl.ds(j * 128, 128)
        k.wg_src[at] = jnp.transpose(k.w_gate_in[:, at])
        k.wu_src[at] = jnp.transpose(k.w_up_in[:, at])

    query_gain = jnp.transpose(jnp.broadcast_to(k.query_gain_in[...], (128, hd)))[:, :1]
    key_gain = jnp.transpose(jnp.broadcast_to(k.key_gain_in[...], (128, hd)))[:, :1]
    adv(main, main, main)
    cot_steps = begin(gather_steps(node, k.g_cot, sems("ag_cot"), 1, 1))
    finish(main)
    finish(wa_steps)
    rates_end(k.wide0, k.rates_in, rate_copies)
    wg_steps = begin(weight_steps(node, k.wg_src, k.wg, sems("wg")))
    adv(cot_steps)
    def project(j):
        cols = span(j, tile)
        acc = nt(k.wa[0, 0 : 3 * hd], k.g_in[0, cols])
        for i in range(1, rows_n):
            acc = acc + nt(k.wa[i, 0 : 3 * hd], k.g_in[i, cols])
        k.raw[:, cols] = acc * k.rates_in[0:1, cols]

    tiles(project)
    adv(cot_steps)
    raw_query, raw_key = k.raw[0:hd], k.raw[hd : 2 * hd]
    cos, sin = k.cos[...], k.sin[...]

    def rotated(raw, gain):
        rate = lax.rsqrt(jnp.mean(raw * raw, axis=0, keepdims=True) + epsilon)
        scaled = raw * rate * gain
        a, b = scaled[: hd // 2], scaled[hd // 2 :]
        return jnp.concatenate([a * cos - b * sin, b * cos + a * sin], axis=0)

    k.qt[...] = rotated(raw_query, query_gain).astype(LOW)
    key_turned = rotated(raw_key, key_gain)
    value_turned = k.raw[2 * hd :]
    k.kt[...] = key_turned.astype(LOW)
    k.vt[...] = value_turned.astype(LOW)
    k.kn[...] = jnp.transpose(key_turned).astype(LOW)
    k.vn[...] = jnp.transpose(value_turned).astype(LOW)
    for j in range(length // tile):
        cols = pl.ds(j * tile, tile)
        ext = (j + 1) * tile
        scores = nn(k.kn[0:ext], k.qt[:, cols]) * scale
        at = lax.broadcasted_iota(jnp.int32, (ext, tile), 0)
        own_place = lax.broadcasted_iota(jnp.int32, (ext, tile), 1) + j * tile
        allowed = (at >= k.start[0:1, cols]) & (at <= own_place)
        raised = jnp.where(allowed, jnp.exp(scores), 0.0)
        probs = raised * (1.0 / jnp.sum(raised, axis=0, keepdims=True))
        k.probs[0:ext, cols] = probs
        k.mixt[:, cols] = nn(k.vt[:, 0:ext], probs.astype(LOW))
        adv(cot_steps)
    k.mix[...] = jnp.transpose(k.mixt[...]).astype(LOW)
    def out_part(r):
        def body(j):
            rows = span(j, tile)
            k.part[r, rows] = nn(k.mix[rows], k.wa[r, 3 * hd :]).astype(LOW)

        tiles(body)

    def take(total):
        k.blk[...] = total

    def bufs(name, second=""):
        return (
            getattr(k, "part" + second),
            getattr(k, name + "_got"),
            getattr(k, "passed" + second),
            getattr(k, name + "_far"),
            getattr(k, "leave" + second),
            getattr(k, name + "_arr"),
            getattr(k, "carry" + second),
        )

    main = begin(reduce_steps(node, bufs("ro"), sems("ro"), 2, out_part, take))
    adv(main, main, main, main, main, main, main)
    wu_steps = begin(weight_steps(node, k.wu_src, k.wu, sems("wu")))
    adv(cot_steps)
    adv(main, main)
    adv(cot_steps)
    adv(main, main)
    adv(cot_steps)
    wd_steps = begin(weight_steps(node, k.w_down_in, k.wd, sems("wd")))
    finish(main)
    resid = k.hidden_in[...] + k.blk[...]
    k.resid[...] = resid
    stat_copies = row_stat_start(node, k.stat1, row_sums(resid * resid), sems("stat1"))
    k.g_mid[node.r, mine] = (resid * k.norm_mid_in[...]).astype(LOW)
    def ff_in(r, i):
        def body(j):
            cols = span(j, tile)
            gate = nt(k.wg[r], k.g_mid[r, cols])
            up = nt(k.wu[r], k.g_mid[r, cols])
            if i:
                gate = gate + k.gate[:, cols]
                up = up + k.up[:, cols]
            k.gate[:, cols] = gate
            k.up[:, cols] = up

        tiles(body)

    def mid_done(r, i):
        if i == 0:
            finish(wg_steps)
            finish(wu_steps)
        if i == 2:
            finish(wd_steps)
            finish(cot_steps)

            def body(j):
                cols = span(j, tile)
                acc = nt(k.wd[0], k.g_cot[0, cols])
                for i in range(1, rows_n):
                    acc = acc + nt(k.wd[i], k.g_cot[i, cols])
                k.gsw[:, cols] = acc

            tiles(body)
        ff_in(r, i)

    main = begin(gather_steps(node, k.g_mid, sems("ag_mid"), 2, 3, mid_done))
    rates = lax.rsqrt(row_stat_end(k.stat1, stat_copies) / model + epsilon)
    k.rate_mid[...] = jnp.broadcast_to(to_column(rates), k.rate_mid.shape)
    rate_copies = rates_start(node, k.wide1, rates, sems("stat1"))
    adv(wg_steps, wg_steps, wg_steps, cot_steps)
    adv(main)
    adv(wu_steps, wu_steps, wu_steps, cot_steps)
    adv(main, main, main)
    adv(wd_steps, wd_steps, wd_steps, cot_steps)
    finish(main)
    rates_end(k.wide1, k.rates_mid, rate_copies)
    def activate(j):
        cols = span(j, tile)
        rate = k.rates_mid[0:1, cols]
        gate, up, gsw = k.gate[:, cols] * rate, k.up[:, cols] * rate, k.gsw[:, cols]
        sig = 1.0 / (1.0 + jnp.exp(-gate))
        act = gate * sig
        sw = act * up
        gga = gsw * up * sig * (1.0 + gate * (1.0 - sig))
        gua = gsw * act
        k.sw[:, cols] = sw.astype(LOW)
        k.gga[:, cols] = (gga * rate).astype(LOW)
        k.gua[:, cols] = (gua * rate).astype(LOW)
        k.sw_t[cols] = jnp.transpose(sw).astype(LOW)
        k.gga_t[cols] = jnp.transpose(gga).astype(LOW)
        k.gua_t[cols] = jnp.transpose(gua).astype(LOW)

    tiles(activate)
    def mid_part(r):
        def body(j):
            rows = span(j, tile)
            k.part[r, rows] = (nn(k.gga_t[rows], k.wg[r]) + nn(k.gua_t[rows], k.wu[r])).astype(LOW)

        tiles(body)

    def down_part(r):
        def body(j):
            rows = span(j, tile)
            k.part2[r, rows] = nn(k.sw_t[rows], k.wd[r]).astype(LOW)

        tiles(body)

    def outer(left, whole, target):
        def start():
            def body(i, _):
                target[i] = nn(left[...], whole[i]).astype(LOW)
                return 0

            lax.fori_loop(0, rows_n, body, 0)

        return start

    def turned_out(source, target, name):
        def done():
            for j in range(rows_n * units // 128):
                at = pl.ds(j * 128, 128)
                target[:, at] = jnp.transpose(source[at].astype(FLT))
            store(name)

        return done

    def down_out():
        k.f_grad_down[...] = k.od[...].astype(FLT)
        store("grad_down")

    gd_steps = grad_steps(
        node, k.gs_d, k.yb_d, k.gr_d, k.od, sems("gd"), outer(k.sw, k.g_cot, k.gs_d), down_out
    )
    gg_steps = grad_steps(
        node, k.gs_g, k.yb_g, k.gr_g, k.og, sems("gg"), outer(k.gga, k.g_mid, k.gs_g),
        turned_out(k.og, k.f_grad_gate, "grad_gate"),
    )
    gu_steps = grad_steps(
        node, k.gs_u, k.yb_u, k.gr_u, k.ou, sems("gu"), outer(k.gua, k.g_mid, k.gs_u),
        turned_out(k.ou, k.f_grad_up, "grad_up"),
    )

    def put_output(total):
        k.f_output[...] = k.resid[...] + total
        store("output")

    main = begin(reduce_steps(node, bufs("rm"), sems("rm"), 2, mid_part, take))
    adv(main, main, main, main, main, main, main)
    begin(gd_steps)
    adv(main)
    begin(gg_steps)
    adv(main)
    begin(gu_steps)
    adv(main, main)
    adv(gd_steps)
    adv(main, main)
    finish(main)
    down_steps = reduce_steps(node, bufs("rd", "2"), sems("rd"), 1, down_part, put_output)
    grad_normed_mid = k.blk[...]
    resid = k.resid[...]
    rate_mid = k.rate_mid[:, 0:1]
    scaled = k.norm_mid_in[...] * grad_normed_mid
    total = row_stat_steps(node, k.stat2, row_sums(scaled * resid), sems("stat2"))
    grad_resid = k.cot_in[...] + rate_mid * scaled - resid * (
        rate_mid * rate_mid * rate_mid * to_column(total / model)
    )
    k.grad_resid[...] = grad_resid
    k.g_res[node.r, mine] = grad_resid.astype(LOW)
    main = begin(gather_steps(node, k.g_res, sems("ag_res"), 2, 3))
    begin(down_steps)
    gain_mid = jnp.sum(grad_normed_mid * resid * rate_mid, axis=0, keepdims=True)
    adv(main)
    adv(gg_steps)
    adv(main)
    adv(down_steps, down_steps)
    adv(main, main)
    adv(gd_steps, gu_steps)
    adv(down_steps, down_steps, down_steps)
    adv(main, main, main)
    adv(gg_steps)
    finish(main)
    def grad_mixed(j):
        cols = span(j, tile)
        acc = nt(k.wa[0, 3 * hd :], k.g_res[0, cols])
        for i in range(1, rows_n):
            acc = acc + nt(k.wa[i, 3 * hd :], k.g_res[i, cols])
        k.gmt[:, cols] = acc.astype(LOW)

    tiles(grad_mixed)
    k.dk[...] = jnp.zeros(k.dk.shape, FLT)
    k.dv[...] = jnp.zeros(k.dv.shape, FLT)
    for j in range(length // tile):
        cols = pl.ds(j * tile, tile)
        ext = (j + 1) * tile
        probs = k.probs[0:ext, cols]
        k.dv[:, 0:ext] += nt(k.gmt[:, cols], probs.astype(LOW))
        grad_probs = nn(k.vn[0:ext], k.gmt[:, cols])
        inner = jnp.sum(probs * grad_probs, axis=0, keepdims=True)
        grad_scores = (probs * (grad_probs - inner) * scale).astype(LOW)
        k.dq[:, cols] = nn(k.kt[:, 0:ext], grad_scores)
        k.dk[:, 0:ext] += nt(k.qt[:, cols], grad_scores)
        adv(down_steps)

    def turned_back(grad, raw, gain):
        rate = lax.rsqrt(jnp.mean(raw * raw, axis=0, keepdims=True) + epsilon)
        a, b = grad[: hd // 2], grad[hd // 2 :]
        t = jnp.concatenate([a * cos + b * sin, b * cos - a * sin], axis=0)
        scaled = gain * t
        inner = jnp.mean(scaled * raw, axis=0, keepdims=True)
        return (
            rate * scaled - raw * (rate * rate * rate * inner),
            jnp.sum(t * raw * rate, axis=1, keepdims=True),
        )

    cos, sin = k.cos[...], k.sin[...]
    grad_query, gain_query = turned_back(k.dq[...], k.raw[0:hd], query_gain)
    grad_key, gain_key = turned_back(k.dk[...], k.raw[hd : 2 * hd], key_gain)
    grad_proj = jnp.concatenate([grad_query, grad_key, k.dv[...]], axis=0)
    k.gp_turned[...] = (grad_proj * k.rates_in[0:1]).astype(LOW)
    k.gp[...] = jnp.transpose(grad_proj).astype(LOW)
    def in_part(r):
        def body(j):
            rows = span(j, tile)
            k.part[r, rows] = nn(k.gp[rows], k.wa[r, 0 : 3 * hd]).astype(LOW)

        tiles(body)

    def outer_attention():
        def body(i, _):
            k.gs_a[i, 0 : 3 * hd] = nn(k.gp_turned[...], k.g_in[i]).astype(LOW)
            k.gs_a[i, 3 * hd :] = nn(k.mixt[...].astype(LOW), k.g_res[i]).astype(LOW)
            return 0

        lax.fori_loop(0, rows_n, body, 0)

    def attention_out():
        def part(r, i):
            return k.oa[r * width + i * hd : r * width + (i + 1) * hd].astype(FLT)

        k.f_grad_query[...] = jnp.transpose(
            jnp.concatenate([part(r, 0) for r in range(rows_n)], axis=0)
        )
        for i, target in ((1, k.f_grad_key), (2, k.f_grad_value)):
            heads = []
            for h in range(rows_n // share):
                acc = part(h * share, i)
                for r in range(h * share + 1, (h + 1) * share):
                    acc = acc + part(r, i)
                heads.append(acc)
            target[...] = jnp.transpose(jnp.concatenate(heads, axis=0))
        for r in range(rows_n):
            k.f_grad_out[r * hd : (r + 1) * hd] = part(r, 3)
        for name in ("grad_query", "grad_key", "grad_value", "grad_out"):
            store(name)

    ga_steps = grad_steps(
        node, k.gs_a, k.yb_a, k.gr_a, k.oa, sems("ga"), outer_attention, attention_out
    )
    main = begin(reduce_steps(node, bufs("ri"), sems("ri"), 2, in_part, take))
    k.gains[...] = jnp.zeros(k.gains.shape, FLT)
    k.gains[0:1, :] = gain_mid
    k.gains[1:2, 0:hd] = to_row(gain_query)
    k.gains[2:3, 0:hd] = to_row(gain_key)
    gain_copies = group_sum_start(node, k.gbox, k.gains[...], sems("gbox"))
    adv(main, main, main, main, main, main, main)
    begin(ga_steps)
    adv(gu_steps)
    adv(main, main)
    adv(ga_steps)
    adv(main, main)
    adv(gd_steps, gg_steps, gu_steps)
    adv(main, main)
    finish(main)
    adv(ga_steps)
    grad_normed_in = k.blk[...]
    rate_in = k.rate_in[:, 0:1]
    hidden = k.hidden_in[...]
    gain_in = jnp.sum(grad_normed_in * hidden * rate_in, axis=0, keepdims=True)
    in_copies = group_sum_start(
        node, k.inbox, jnp.broadcast_to(gain_in, k.gains.shape), sems("inbox")
    )
    for copy in gain_copies:
        copy.wait_recv()
    gains = box_total(k.gbox)
    k.f_gain_mid[...] = gains[0:1]
    store("gain_mid")
    k.qkbox[node.r] = gains
    qk_copies = [
        node.send(k.qkbox.at[node.r], k.qkbox.at[node.r], sems("qkbox"), s - 1, row=node.row(s))
        for s in (1, 2, 3)
    ]
    scaled = k.norm_in_in[...] * grad_normed_in
    total = row_stat_steps(node, k.stat3, row_sums(scaled * hidden), sems("stat3"))
    k.f_grad_hidden[...] = (
        k.grad_resid[...] + rate_in * scaled - hidden * (rate_in * rate_in * rate_in * to_column(total / model))
    )
    store("grad_hidden")
    finish(down_steps)
    for steps in (gd_steps, gg_steps, gu_steps, ga_steps):
        finish(steps)
    for copy in qk_copies:
        copy.wait_recv()
    gains = box_total(k.qkbox)
    k.f_gain_query[...] = gains[1:2, 0:hd]
    k.f_gain_key[...] = gains[2:3, 0:hd]
    store("gain_query")
    store("gain_key")
    for copy in in_copies:
        copy.wait_recv()
    k.f_gain_in[...] = box_total(k.inbox)[0:1]
    store("gain_in")
    for copy in gain_copies + qk_copies + in_copies:
        copy.wait_send()
    for copy in stores:
        copy.wait()


def copy_kernel(count, *refs):
    held, arrive, leave = refs[2 * count : 3 * count], refs[-2], refs[-1]
    inward = [pltpu.make_async_copy(refs[i], held[i], arrive.at[i]) for i in range(count)]
    outward = [
        pltpu.make_async_copy(held[i], refs[count + i], leave.at[i]) for i in range(count)
    ]
    for copy in inward:
        copy.start()
    for came, left in zip(inward, outward):
        came.wait()
        left.start()
    for copy in outward:
        copy.wait()


SMALL = ("norm_in", "segments", "frequency", "query_gain", "key_gain", "norm_mid")
LARGE = ("w_query", "w_key", "w_value", "w_out", "cot", "w_gate", "w_up", "w_down")
LOADED = ("hidden",) + SMALL + LARGE


def local(
    hidden_in,
    segments,
    norm_in,
    w_query,
    w_key,
    w_value,
    query_gain,
    key_gain,
    w_out,
    norm_mid,
    w_gate,
    w_up,
    w_down,
    cotangent,
):
    rows, cols, dps = lax.axis_size("row"), lax.axis_size("col"), lax.axis_size("dp")
    pair = dps == 2
    slab, feat = hidden_in.shape
    length = segments.shape[1]
    hd = HEAD_DIM
    q_cols, k_cols, u_cols = w_query.shape[1], w_key.shape[1], w_gate.shape[1]
    share = rows * hd // k_cols
    units = u_cols // rows
    assert rows == 4 and cols == 4 and q_cols == rows * hd and slab * cols == length
    dims = SimpleNamespace(
        slab=slab, feat=feat, length=length, units=units, share=share, rows=rows
    )
    powers = np.arange(hd // 2, dtype=np.float64) * (-2.0 / hd)
    frequency = jnp.asarray((rope_base**powers).astype(np.float32)[:, None])
    shape = jax.ShapeDtypeStruct
    small = dict(
        segments=segments,
        norm_in=norm_in[None, :],
        norm_mid=norm_mid[None, :],
        query_gain=query_gain[None, :],
        key_gain=key_gain[None, :],
        frequency=frequency,
    )
    large = dict(
        hidden=hidden_in,
        cot=cotangent,
        w_query=w_query,
        w_key=w_key,
        w_value=w_value,
        w_out=w_out,
        w_gate=w_gate,
        w_up=w_up,
        w_down=w_down,
    )
    block = (slab, feat)
    large_outs = dict(
        output=block,
        grad_hidden=block,
        grad_query=w_query.shape,
        grad_key=w_key.shape,
        grad_value=w_value.shape,
        grad_out=w_out.shape,
        grad_gate=w_gate.shape,
        grad_up=w_up.shape,
        grad_down=w_down.shape,
    )
    small_outs = dict(
        gain_mid=(1, feat), gain_in=(1, feat), gain_query=(1, hd), gain_key=(1, hd)
    )
    width = 4 * hd
    low = lambda *dims: pltpu.VMEM(dims, LOW)
    flt = lambda *dims: pltpu.VMEM(dims, FLT)
    group = cols * (2 if pair else 1)
    scratch = {
        name + "_in": pltpu.VMEM(array.shape, array.dtype)
        for name, array in (small | large).items()
    }
    scratch.update({"f_" + name: flt(*dims) for name, dims in (small_outs | large_outs).items()})
    scratch.update(
        loads=pltpu.SemaphoreType.DMA((len(LOADED),)),
        stores=pltpu.SemaphoreType.DMA((len(small_outs) + len(large_outs),)),
        wa_src=low(rows * width, feat),
        wg_src=low(rows * units, feat),
        wu_src=low(rows * units, feat),
        resid=flt(slab, feat),
        grad_resid=flt(slab, feat),
        blk=flt(slab, feat),
        carry=flt(slab, feat),
        carry2=flt(slab, feat),
        rate_in=flt(slab, 128),
        rate_mid=flt(slab, 128),
        start=pltpu.VMEM((8, length), jnp.int32),
        rates_in=flt(8, length),
        rates_mid=flt(8, length),
        wide0=flt(cols, 8, slab),
        wide1=flt(cols, 8, slab),
        cos=flt(hd // 2, length),
        sin=flt(hd // 2, length),
        wa=low(rows, width, feat),
        wg=low(rows, units, feat),
        wu=low(rows, units, feat),
        wd=low(rows, units, feat),
        part=low(rows, length, feat),
        part2=low(rows, length, feat),
        passed=low(rows, slab, feat),
        passed2=low(rows, slab, feat),
        leave=low(rows - 1, slab, feat),
        leave2=low(rows - 1, slab, feat),
        raw=flt(3 * hd, length),
        qt=low(hd, length),
        kt=low(hd, length),
        vt=low(hd, length),
        kn=low(length, hd),
        vn=low(length, hd),
        probs=flt(length, length),
        mixt=flt(hd, length),
        mix=low(length, hd),
        gmt=low(hd, length),
        dq=flt(hd, length),
        dk=flt(hd, length),
        dv=flt(hd, length),
        gp_turned=low(3 * hd, length),
        gp=low(length, 3 * hd),
        gate=flt(units, length),
        up=flt(units, length),
        gsw=flt(units, length),
        sw=low(units, length),
        gga=low(units, length),
        gua=low(units, length),
        sw_t=low(length, units),
        gga_t=low(length, units),
        gua_t=low(length, units),
        gains=flt(8, feat),
        gbox=flt(group, 8, feat),
        inbox=flt(group, 8, feat),
        qkbox=flt(rows, 8, feat),
    )
    counts = dict(gbox=group - 1, inbox=group - 1, qkbox=3)
    for name in ("stat0", "stat1", "stat2", "stat3"):
        scratch[name] = flt(rows, 8, slab)
        counts[name] = 6 if name in ("stat0", "stat1") else 3
    for name in ("in", "cot", "mid", "res"):
        scratch["g_" + name] = low(rows, length, feat)
        counts["ag_" + name] = 17 * (1 if name == "cot" else 2)
    for name in ("ro", "rm", "rd", "ri"):
        scratch[name + "_got"] = low(rows, 2, slab, feat)
        scratch[name + "_far"] = low(rows, slab, feat)
        scratch[name + "_arr"] = low(rows + 1, slab, feat)
        pieces = 1 if name == "rd" else 2
        counts[name] = 13 * pieces + 4
    for name, size in (("a", width), ("g", units), ("u", units), ("d", units)):
        half = size // 2 if pair else size
        scratch["gs_" + name] = low(rows, size, feat)
        scratch["yb_" + name] = low(rows, half, feat)
        scratch["gr_" + name] = low(rows, half, feat)
        scratch["o" + name] = low(rows * size, feat)
        counts["w" + name] = 6
        counts["g" + name] = 8
    for name, count in counts.items():
        scratch[name + "_send"] = pltpu.SemaphoreType.DMA((count,))
        scratch[name + "_recv"] = pltpu.SemaphoreType.DMA((count,))
    anywhere = pl.BlockSpec(memory_space=pl.ANY)
    names = tuple(small) + tuple(large) + tuple(small_outs) + tuple(large_outs) + tuple(scratch)
    out_shape = tuple(shape(d, FLT) for d in (small_outs | large_outs).values())
    got = pl.pallas_call(
        functools.partial(kernel, dims, pair, names),
        out_shape=out_shape,
        in_specs=[anywhere] * (len(small) + len(large)),
        out_specs=(anywhere,) * len(out_shape),
        scratch_shapes=list(scratch.values()),
        compiler_params=pltpu.CompilerParams(
            collective_id=0, has_side_effects=True, vmem_limit_bytes=60 * 2**20
        ),
    )(*small.values(), *large.values())
    if pair:
        got = pl.pallas_call(
            functools.partial(copy_kernel, len(got)),
            out_shape=out_shape,
            in_specs=[anywhere] * len(got),
            out_specs=(anywhere,) * len(got),
            scratch_shapes=[pltpu.VMEM(array.shape, array.dtype) for array in got]
            + [pltpu.SemaphoreType.DMA((len(got),))] * 2,
        )(*got)
    o = SimpleNamespace(**dict(zip(tuple(small_outs) + tuple(large_outs), got, strict=True)))
    if not pair:
        for name in tuple(small_outs) + tuple(large_outs)[2:]:
            setattr(o, name, lax.psum(getattr(o, name), "dp"))
    return (
        o.output,
        o.grad_hidden,
        o.gain_in[0],
        o.grad_query,
        o.grad_key,
        o.grad_value,
        o.gain_query[0],
        o.gain_key[0],
        o.grad_out,
        o.gain_mid[0],
        o.grad_gate,
        o.grad_up,
        o.grad_down,
    )


def solution(mesh):
    stream = P(("dp", "col"), "row")
    first, last = P("row", "col"), P("col", "row")
    return jax.shard_map(
        local,
        mesh=mesh,
        in_specs=(stream, P("dp", None), P("row"), first, first, first, P(), P(), last, P("row"), first, first, last, stream),
        out_specs=(stream, stream, P("row"), first, first, first, P(), P(), last, P("row"), first, first, last),
        check_vma=False,
    )
```
